32 devices in a mesh: gx: 8 (over z, x), gy: 4 (over y, core).
Axes of the slice: x: 2, y: 2, z: 4, core: 2. Of those that a mesh axis runs over, the one named last changes fastest.
Arguments:
- adjoint_init: float32 [3, 128, 128, 128], P(None, 'gx', 'gy'), may hold values from -4 to 4
- adjoint_rhs: float32 [3, 128, 128, 128], P(None, 'gx', 'gy'), may hold values from -6 to 6
- jacobian: bfloat16 [7, 3, 3, 128, 128, 128], P(None, None, None, 'gx', 'gy'), may hold values from -1.796875 to 1.796875
- cell_diag: float32 [3, 128, 128, 128], P(None, 'gx', 'gy'), may hold values from 1.5 to 3
- perf_owner: int32 [8192, 1], P(('gx', 'gy')), may hold values from 0 to 3; in each aligned block of 256 rows (0 to 255, 256 to 511, ...) at most 64 rows name the same one
- perf_well: int32 [8192], P(('gx', 'gy')), may hold values from 0 to 31
- perf_block: int32 [8192], P(('gx', 'gy')), may hold values from 0 to 1023
- well_coupling: bfloat16 [4, 192, 8192], P(None, None, ('gx', 'gy')), may hold values from -0.4375 to 0.4375
- cell_coupling: bfloat16 [4, 192, 8192], P(None, None, ('gx', 'gy')), may hold values from -0.29882812 to 0.29882812
- well_rhs: float32 [4, 1024], P(None, ('gx', 'gy')), may hold values from -6 to 6
- well_inverse: float32 [4, 4, 1024], P(None, None, ('gx', 'gy')), may hold values from -1.5 to 1.5
Outputs:
- adjoint: float32 [3, 128, 128, 128], P(None, 'gx', 'gy')
- well_adjoint: float32 [4, 1024], P(None, ('gx', 'gy'))
The draws below stay inside these ranges and needn't reach their ends.
Inputs may be any that keep to these rules, and one draw needn't show every extreme that they name: `perf_owner`: the owner is a gy index within the perforation's own gx row. Among the 256 perforations of one device no owner is named more than 64 times, and in some device one owner is named exactly 64 times. `perf_block`: block of the perforating device's own cells, numbered as in the reference program.
All inputs are finite; a program needn't handle non-finite values.
Results may differ from the reference program's by a relative error of at most 0.0004.
Values may be sent and summed in bfloat16 or wider, within the bound.
No kernel may reach another device: no remote copies, remote signals or barrier semaphores. Data moves between devices by JAX's collectives and lax.ppermute only.
A program may use at most 128 MiB of HBM per device.

```python
import math
import jax
import jax.numpy as jnp
import numpy as np
from jax import lax

PHASES = 3
WELL_UNK = 4
BLOCK = 64
ITERS = 8
CX = 16
CY = 32
NZ = 128
PERF_DEV = 256
CAP = 64
WELL_DEV = 32
NX = 128
NY = 128
NZB = 2
BLK_DEV = 1024
PERFS = 8192
WELLS = 1024
N_GY = 4


def with_ends(values, own_key, least, largest):
    place = [jax.random.randint(jax.random.fold_in(own_key, axis), (), 0, length) for axis, length in enumerate(values.shape)]
    widest = values.shape.index(max(values.shape))
    next_to = place[:widest] + [(place[widest] + 1) % values.shape[widest]] + place[widest + 1:]
    return values.at[tuple(place)].set(least).at[tuple(next_to)].set(largest)


def levels(own_key, dims, shards, smallest, largest):
    def one(axis_at, parts):
        draws = jax.random.uniform(jax.random.fold_in(jax.random.fold_in(own_key, 6), axis_at), (parts,), jnp.float32, smallest / len(shards), largest / len(shards))
        return jnp.repeat(jnp.exp(draws), dims[axis_at] // parts).reshape((-1,) + (1,) * (len(dims) - axis_at - 1))

    loudness = one(*shards[0])
    for cut in shards[1:]:
        loudness = loudness * one(*cut)
    return loudness


def shared_out(key, own, number, rows, number_of, top, reach, lean):
    order = jax.random.permutation(key, number_of)
    packed, ordinary = load_shares(number_of, rows * top, reach, lean, True), load_shares(number_of, rows * top, reach, lean, False)
    places = jnp.arange(number_of)

    def named(tallies, turn):
        used = int((tallies > 0).sum())
        fixed = max(1, used // 4)
        moved = fixed + (places - fixed + turn * (used - fixed)) % max(1, number_of - fixed)
        return jnp.zeros((number_of,), jnp.int32).at[order[jnp.where(places < fixed, places, moved)]].set(jnp.asarray(tallies, jnp.int32))

    tallies = jnp.where(number % 4 == 0, named(packed, number // 4), named(ordinary, number - number // 4 - 1))
    mixed = jax.random.permutation(jax.random.fold_in(own, 3), number_of)
    giver, sink = mixed[0:number_of // 2 * 2:2], mixed[1:number_of // 2 * 2:2]
    room = jnp.minimum(tallies[giver] - 1, reach - tallies[sink]) // 2
    room = jnp.where((giver == order[0]) | (sink == order[0]) | (tallies[sink] == 0), 0, jnp.maximum(room, 0))
    moved = jax.random.randint(jax.random.fold_in(own, 4), (number_of // 2,), 0, 1 << 20) % (room + 1)
    tallies = tallies.at[giver].add(-moved).at[sink].add(moved)
    members = jnp.searchsorted(jnp.cumsum(tallies), jnp.arange(rows * top), side="right").astype(jnp.int32)
    grid = members.reshape(top, rows).T
    grid = grid[jax.random.permutation(jax.random.fold_in(own, 1), rows)]
    turn = jax.random.randint(jax.random.fold_in(own, 2), (rows, 1), 0, top)
    return jnp.take_along_axis(grid, (jnp.arange(top)[None, :] + turn) % top, axis=1)


def load_shares(count, total, reach, lean, full):
    portions = [(1 << 20) // math.isqrt(rank ** lean) + 1 for rank in range(1, count + 1)]
    largest = reach if full else min(reach, max(-(-total // count), total * portions[0] // sum(portions)))
    least = 1 if total - largest >= count - 1 else 0
    counts, spare = [largest] + [least] * (count - 1), total - largest - least * (count - 1)
    while spare > 0:
        free = [i for i in range(1, count) if counts[i] < largest] or [i for i in range(1, count) if counts[i] < reach]
        whole, budget = sum([portions[i] for i in free]), spare
        for i in free:
            more = min(reach - counts[i], max(1, budget * portions[i] // whole), spare)
            counts[i] = counts[i] + more
            spare = spare - more
    return np.array(counts)


def scatter_about(rng, extent, deviation, bound, shards=(), held_as=jnp.bfloat16):
    level = levels(rng, extent, shards, -0.22, 0.18) if shards else 1.0
    array = jax.random.normal(rng, extent, jnp.float32) * deviation * level
    return jnp.minimum(jnp.maximum(array, -bound), bound).astype(held_as)


def setup_inputs(seed: int = 0) -> dict:
    seeds = jax.random.split(jax.random.key(seed), 12)
    adjoint_init = scatter_about(seeds[0], (PHASES, NX, NY, NZ), 0.5, 4.0, ((1, 8), (2, 4)), jnp.float32)
    adjoint_rhs = scatter_about(seeds[1], (PHASES, NX, NY, NZ), 1.0, 6.0, ((1, 8), (2, 4)), jnp.float32)
    jacobian = scatter_about(seeds[2], (7, PHASES, PHASES, NX, NY, NZ), 0.3, 1.796875, ((3, 8), (4, 4)))
    cell_diag = jnp.clip(1.5 + 1.5 * jax.random.uniform(seeds[3], (PHASES, NX, NY, NZ), jnp.float32) ** levels(seeds[3], (PHASES, NX, NY, NZ), ((1, 8), (2, 4)), -0.2, 0.2), 1.5, 3.0)
    perf_owner_keys = jax.random.split(jax.random.fold_in(seeds[4], 1), PERFS // PERF_DEV)
    perf_owner_turns = jax.random.permutation(jax.random.fold_in(seeds[4], 3), PERFS // PERF_DEV)
    perf_owner = jax.vmap(lambda own, number: shared_out(jax.random.fold_in(seeds[4], 2), own, number, PERF_DEV, N_GY, 1, CAP, 2))(perf_owner_keys, perf_owner_turns).reshape((PERFS, 1))
    perf_well = with_ends(jax.random.randint(seeds[5], (PERFS,), 0, WELL_DEV), jax.random.fold_in(seeds[5], 1), 0, WELL_DEV - 1).astype(jnp.int32)
    perf_block = with_ends(jax.random.randint(seeds[6], (PERFS,), 0, BLK_DEV), jax.random.fold_in(seeds[6], 1), 0, BLK_DEV - 1).astype(jnp.int32)
    well_coupling = scatter_about(seeds[7], (WELL_UNK, PHASES * BLOCK, PERFS), (PHASES * BLOCK) ** -0.5, 0.4375, ((2, 32),))
    cell_coupling = scatter_about(seeds[8], (WELL_UNK, PHASES * BLOCK, PERFS), 0.05, 0.29882812, ((2, 32),))
    well_rhs = scatter_about(seeds[9], (WELL_UNK, WELLS), 1.0, 6.0, ((1, 32),), jnp.float32)
    well_inverse = scatter_about(seeds[10], (WELL_UNK, WELL_UNK, WELLS), 16 ** -0.5, 1.5, ((2, 32),), jnp.float32)
    return dict(adjoint_init=adjoint_init, adjoint_rhs=adjoint_rhs, jacobian=jacobian, cell_diag=cell_diag, perf_owner=perf_owner, perf_well=perf_well, perf_block=perf_block, well_coupling=well_coupling, cell_coupling=cell_coupling, well_rhs=well_rhs, well_inverse=well_inverse)


neighbour_moves = [(1, 1), (1, -1), (2, 1), (2, -1), (3, 1), (3, -1)]


def shifted(values, axis_index, offset):
    length = values.shape[axis_index]
    border_shape = list(values.shape)
    border_shape[axis_index] = 1
    border = jnp.zeros(border_shape, values.dtype)
    if offset > 0:
        return jnp.concatenate([lax.slice_in_dim(values, 1, length, axis=axis_index), border], axis=axis_index)
    return jnp.concatenate([border, lax.slice_in_dim(values, 0, length - 1, axis=axis_index)], axis=axis_index)


def direction_term(jacobian, current, direction):
    return jnp.stack([sum(jacobian[direction, source, target].astype(jnp.float32) * current[source] for source in range(PHASES)) for target in range(PHASES)])


def transposed_image(jacobian, current, cell_diag):
    summed = cell_diag * current + direction_term(jacobian, current, 0)
    for direction in range(1, 7):
        axis_index, offset = neighbour_moves[direction - 1]
        summed = summed + shifted(direction_term(jacobian, current, direction), axis_index, offset)
    return summed


def well_part(current, perf_owner, perf_well, perf_block, well_coupling, cell_coupling, well_rhs, well_inverse):
    perf_total = perf_well.shape[0]
    perf_index = jnp.arange(perf_total, dtype=jnp.int32)
    device = perf_index // PERF_DEV
    row_dev = device // N_GY
    col_dev = device % N_GY
    cell_row = row_dev * CX + perf_block // (CY * NZB)
    cell_col = col_dev * CY + (perf_block // NZB) % CY
    layer_block = perf_block % NZB
    grid_blocks = current.reshape(PHASES, NX, NY, NZB, BLOCK)
    picked = grid_blocks[:, cell_row, cell_col, layer_block, :]
    block_rows = jnp.transpose(picked, (0, 2, 1)).reshape(PHASES * BLOCK, perf_total)
    perf_terms = jnp.sum(well_coupling.astype(jnp.float32) * block_rows[None], axis=1)
    target_well = (row_dev * N_GY + perf_owner[:, 0]) * WELL_DEV + perf_well
    well_terms = jax.ops.segment_sum(perf_terms.T, target_well, num_segments=WELLS).T
    well_adjoint = jnp.sum(well_inverse * (well_rhs - well_terms)[:, None, :], axis=0)
    perf_adjoint = well_adjoint[:, target_well]
    coupling_rows = jnp.sum(cell_coupling.astype(jnp.float32) * perf_adjoint[:, None, :], axis=0)
    pieces = jnp.transpose(coupling_rows.reshape(PHASES, BLOCK, perf_total), (0, 2, 1))
    coupling = jnp.zeros((PHASES, NX, NY, NZB, BLOCK), jnp.float32).at[:, cell_row, cell_col, layer_block, :].add(pieces)
    return well_adjoint, coupling.reshape(PHASES, NX, NY, NZ)


def reference(adjoint_init, adjoint_rhs, jacobian, cell_diag, perf_owner, perf_well, perf_block, well_coupling, cell_coupling, well_rhs, well_inverse):
    current = adjoint_init
    well_adjoint = jnp.zeros_like(well_rhs)
    for sweep_index in range(ITERS):
        transposed = transposed_image(jacobian, current, cell_diag)
        well_adjoint, coupling = well_part(current, perf_owner, perf_well, perf_block, well_coupling, cell_coupling, well_rhs, well_inverse)
        current = current + (adjoint_rhs - transposed - coupling) / cell_diag
    return current, well_adjoint
```

```python
import functools

import jax
import jax.numpy as jnp
from jax import lax
from jax.experimental import pallas as pl
from jax.experimental.pallas import tpu as pltpu
from jax.sharding import PartitionSpec as P

PHASES = 3
WELL_UNK = 4
BLOCK = 64
ITERS = 8
LANES = 128
F32 = jnp.float32
BF16 = jnp.bfloat16
VM = pl.BlockSpec(memory_space=pltpu.VMEM)
SM = pl.BlockSpec(memory_space=pltpu.SMEM)
PARAMS = pltpu.CompilerParams(vmem_limit_bytes=24 * 1024 * 1024)


def split_2(value):
    high = value.astype(BF16)
    return high, (value - high.astype(F32)).astype(BF16)


def edge_messages(flags, x_ref, jac_ref, col_ref, m1_ref, m2_ref, m3_ref, m4_ref):
    rows, cols = jac_ref.shape[3], jac_ref.shape[4]
    gx_odd, gy_odd = flags[0] == 1, flags[1] == 1
    x_first = [x_ref[r, 0:cols, :] for r in range(PHASES)]
    x_last = [x_ref[r, (rows - 1) * cols : rows * cols, :] for r in range(PHASES)]
    c_first = [x_ref[r, pl.ds(0, rows, stride=cols), :] for r in range(PHASES)]
    c_last = [x_ref[r, pl.ds(cols - 1, rows, stride=cols), :] for r in range(PHASES)]
    for t in range(PHASES):
        up = sum(jac_ref[1, r, t, 0].astype(F32) * x_first[r] for r in range(PHASES))
        down = sum(jac_ref[2, r, t, rows - 1].astype(F32) * x_last[r] for r in range(PHASES))
        left = sum(col_ref[0, r, t] * c_first[r] for r in range(PHASES))
        right = sum(col_ref[1, r, t] * c_last[r] for r in range(PHASES))
        m3_ref[t * cols : (t + 1) * cols, :] = jnp.where(gx_odd, up, down)
        m4_ref[t * cols : (t + 1) * cols, :] = jnp.where(gx_odd, down, up)
        m1_ref[t * rows : (t + 1) * rows, :] = jnp.where(gy_odd, left, right)
        m2_ref[t * rows : (t + 1) * rows, :] = jnp.where(gy_odd, right, left)


def well_partials(x_ref, pick_ref, well_ref, wc_ref, xs_ref, g_ref, write):
    cells = x_ref.shape[1]
    perfs = pick_ref.shape[0]
    for r in range(PHASES):
        high, low = split_2(x_ref[r])
        xs_ref[0:cells, r * LANES : (r + 1) * LANES] = high
        xs_ref[cells : 2 * cells, r * LANES : (r + 1) * LANES] = low
    g_ref[...] = jnp.dot(pick_ref[...], xs_ref[...], preferred_element_type=F32)
    width = well_ref.shape[0]
    chunk = 64
    totals = [[jnp.zeros((8, LANES), F32) for _ in range(width)] for _ in range(WELL_UNK)]
    for start in range(0, perfs, chunk):
        rows = slice(start, start + chunk)
        picked = [g_ref[rows, r * LANES : (r + 1) * LANES] for r in range(PHASES)]
        for u in range(WELL_UNK):
            lane_terms = sum(wc_ref[u, r, rows].astype(F32) * picked[r] for r in range(PHASES))
            term = jnp.sum(lane_terms, axis=1, keepdims=True)
            for h in range(width):
                spread = well_ref[h, rows, :] * term
                totals[u][h] = totals[u][h] + sum(spread[i : i + 8] for i in range(0, chunk, 8))
    for h in range(width):
        for u in range(WELL_UNK):
            write(h * WELL_UNK + u, jnp.sum(totals[u][h], axis=0, keepdims=True))


def expanded(eye, coupling_ref, u, half, out_ref):
    lane = lax.broadcasted_iota(jnp.int32, (eye.shape[0], LANES), 1)
    own_half = (lane // BLOCK) == half
    for r in range(PHASES):
        piece = coupling_ref[u, r * BLOCK : (r + 1) * BLOCK, :]
        doubled = jnp.concatenate([piece, piece], axis=0)
        turned = lax.dot_general(
            eye, doubled, (((1,), (1,)), ((), ())), preferred_element_type=F32
        )
        out_ref[u, r] = jnp.where(own_half, turned, 0.0).astype(BF16)


def first_kernel(
    flags, x_ref, jac_ref, diag_ref, block_row, block_col, well_col, wcoef, ccoef, wconst,
    inv_ref, col_ref, pick_ref, spread_ref, well_ref, wc_ref, cc_ref,
    m1_ref, m2_ref, m3_ref, m4_ref, xs_ref, g_ref,
):
    rows, cols = jac_ref.shape[3], jac_ref.shape[4]
    cells = rows * cols
    perfs = block_row.shape[1]
    inv_ref[...] = 1.0 / diag_ref[...]
    for r in range(PHASES):
        for t in range(PHASES):
            for i in range(rows):
                edge = jac_ref[3, r, t, i].astype(F32)
                col_ref[0, r, t, i : i + 1, :] = edge[0:1]
                edge = jac_ref[4, r, t, i].astype(F32)
                col_ref[1, r, t, i : i + 1, :] = edge[cols - 1 : cols]
    column = block_row[...] // 2
    cell = lax.broadcasted_iota(jnp.int32, (cells, perfs), 0)
    spread = (cell == column).astype(F32).astype(BF16)
    spread_ref[:, 0:perfs] = spread
    spread_ref[:, perfs : 2 * perfs] = spread
    block = block_col[...]
    cell = lax.broadcasted_iota(jnp.int32, (perfs, cells), 1)
    pick = (cell == block // 2).astype(F32).astype(BF16)
    pick_ref[:, 0:cells] = pick
    pick_ref[:, cells : 2 * cells] = pick
    lane = lax.broadcasted_iota(jnp.int32, (perfs, LANES), 1)
    for h in range(well_ref.shape[0]):
        well_ref[h] = (lane + h * LANES == well_col[...]).astype(F32)
    half = block % 2
    a = lax.broadcasted_iota(jnp.int32, (perfs, perfs), 0)
    b = lax.broadcasted_iota(jnp.int32, (perfs, perfs), 1)
    eye = (a == b).astype(F32).astype(BF16)
    for u in range(WELL_UNK):
        expanded(eye, wcoef, u, half, wc_ref)
        expanded(eye, ccoef, u, half, cc_ref)
    edge_messages(flags, x_ref, jac_ref, col_ref, m1_ref, m2_ref, m3_ref, m4_ref)
    base = PHASES * rows

    def write(row, value):
        m1_ref[base + row : base + row + 1, :] = value

    well_partials(x_ref, pick_ref, well_ref, wc_ref, xs_ref, g_ref, write)
    count = WELL_UNK * well_ref.shape[0]
    m1_ref[base + count :, :] = wconst[...]


def add_kernel(base, kept_ref, own_ref, got_ref, out_ref):
    out_ref[0:base, :] = kept_ref[...]
    out_ref[base:, :] = own_ref[base:, :] + got_ref[base:, :]


def inner_kernel(x_ref, jac_ref, rhs_ref, z_ref):
    rows, cols = jac_ref.shape[3], jac_ref.shape[4]
    lane = lax.broadcasted_iota(jnp.int32, (cols, LANES), 1)
    col = lax.broadcasted_iota(jnp.int32, (cols, LANES), 0)

    def row_body(i, carry):
        before, after = jnp.maximum(i - 1, 0), jnp.minimum(i + 1, rows - 1)
        has_before = (i > 0).astype(F32)
        has_after = (i < rows - 1).astype(F32)

        def load(row):
            start = pl.multiple_of(row * cols, cols)
            return [x_ref[r, pl.ds(start, cols), :] for r in range(PHASES)]

        here = load(i)

        def term(d, t, row, values):
            return sum(jac_ref[d, r, t, row].astype(F32) * values[r] for r in range(PHASES))

        start = pl.multiple_of(i * cols, cols)
        total = [term(0, t, i, here) for t in range(PHASES)]
        values = [v * has_after for v in load(after)]
        total = [total[t] + term(1, t, after, values) for t in range(PHASES)]
        values = [v * has_before for v in load(before)]
        total = [total[t] + term(2, t, before, values) for t in range(PHASES)]
        values = [jnp.where(col == 0, 0.0, v) for v in here]
        total = [
            total[t] + pltpu.roll(term(3, t, i, values), cols - 1, 0) for t in range(PHASES)
        ]
        values = [jnp.where(col == cols - 1, 0.0, v) for v in here]
        total = [total[t] + pltpu.roll(term(4, t, i, values), 1, 0) for t in range(PHASES)]
        values = [jnp.where(lane == 0, 0.0, v) for v in here]
        total = [
            total[t] + pltpu.roll(term(5, t, i, values), LANES - 1, 1) for t in range(PHASES)
        ]
        values = [jnp.where(lane == LANES - 1, 0.0, v) for v in here]
        total = [total[t] + pltpu.roll(term(6, t, i, values), 1, 1) for t in range(PHASES)]
        for t in range(PHASES):
            z_ref[t, pl.ds(start, cols), :] = rhs_ref[t, pl.ds(start, cols), :] - total[t]
        return carry

    lax.fori_loop(0, rows, row_body, 0)


def update_kernel(
    last, flags, z_ref, own, g1, g2, g3, g4, wconst, inv_ref, spread_ref, well_ref, cc_ref,
    *rest,
):
    if last:
        x_ref, adj_ref, rs_ref, c_ref = rest
    else:
        (jac_ref, col_ref, pick_ref, wc_ref, x_ref, m1_ref, m2_ref, m3_ref, m4_ref,
         rs_ref, c_ref, xs_ref, g_ref) = rest
    cells, perfs = spread_ref.shape[0], spread_ref.shape[1] // 2
    rows = (own.shape[0] - WELL_UNK * well_ref.shape[0]) // PHASES
    cols = cells // rows
    base = PHASES * rows
    width = well_ref.shape[0]
    unk = WELL_UNK * width
    terms = own[base : base + unk, :] + g2[base : base + unk, :]
    left = wconst[0:unk, :] - terms
    solved = []
    for h in range(width):
        value = 0.0
        for v in range(WELL_UNK):
            at = unk + (h * WELL_UNK + v) * WELL_UNK
            at_v = h * WELL_UNK + v
            value = value + wconst[at : at + WELL_UNK, :] * left[at_v : at_v + 1, :]
        solved.append(value)
    if last:
        for h in range(width):
            adj_ref[h] = solved[h]
    chunk = 64
    for start in range(0, perfs, chunk):
        part = slice(start, start + chunk)
        value = [0.0] * PHASES
        for u in range(WELL_UNK):
            chosen = sum(well_ref[h, part, :] * solved[h][u : u + 1, :] for h in range(width))
            factor = jnp.sum(chosen, axis=1, keepdims=True)
            for r in range(PHASES):
                value[r] = value[r] + cc_ref[u, r, part].astype(F32) * factor
        for r in range(PHASES):
            high, low = split_2(value[r])
            rs_ref[start : start + chunk, r * LANES : (r + 1) * LANES] = high
            rs_ref[perfs + start : perfs + start + chunk, r * LANES : (r + 1) * LANES] = low
    c_ref[...] = jnp.dot(spread_ref[...], rs_ref[...], preferred_element_type=F32)
    gx_odd, gy_odd = flags[0] == 1, flags[1] == 1
    gx_open, gy_open = flags[2].astype(F32), flags[3].astype(F32)
    for t in range(PHASES):
        x_ref[t] = (z_ref[t] - c_ref[:, t * LANES : (t + 1) * LANES]) * inv_ref[t]
    for t in range(PHASES):
        near, far = g3[t * cols : (t + 1) * cols, :], g4[t * cols : (t + 1) * cols, :] * gx_open
        first, final = slice(0, cols), slice((rows - 1) * cols, rows * cols)
        x_ref[t, first, :] = x_ref[t, first, :] - inv_ref[t, first, :] * jnp.where(gx_odd, near, far)
        x_ref[t, final, :] = x_ref[t, final, :] - inv_ref[t, final, :] * jnp.where(gx_odd, far, near)
        near, far = g1[t * rows : (t + 1) * rows, :], g2[t * rows : (t + 1) * rows, :] * gy_open
        first, final = pl.ds(0, rows, stride=cols), pl.ds(cols - 1, rows, stride=cols)
        x_ref[t, first, :] = x_ref[t, first, :] - inv_ref[t, first, :] * jnp.where(gy_odd, near, far)
        x_ref[t, final, :] = x_ref[t, final, :] - inv_ref[t, final, :] * jnp.where(gy_odd, far, near)
    if not last:
        edge_messages(flags, x_ref, jac_ref, col_ref, m1_ref, m2_ref, m3_ref, m4_ref)

        def write(row, value):
            m1_ref[base + row : base + row + 1, :] = value

        well_partials(x_ref, pick_ref, well_ref, wc_ref, xs_ref, g_ref, write)


def gx_swap(gx, gy, parity):
    pairs = []
    for i in range(gx):
        k = i ^ 1 if parity == 0 else ((i + 1) ^ 1) - 1
        for j in range(gy):
            pairs.append((i * gy + j, k * gy + j if 0 <= k < gx else i * gy + (j ^ 1)))
    return pairs


def gy_swap(gy, parity):
    if parity == 0:
        return [(j, j ^ 1) for j in range(gy)]
    return [(j, (((j + 1) ^ 1) - 1) % gy) for j in range(gy)]


def shape(*dims, dtype=F32):
    return jax.ShapeDtypeStruct(dims, dtype)


def body(
    adjoint_init, adjoint_rhs, jacobian, cell_diag, perf_owner, perf_well, perf_block,
    well_coupling, cell_coupling, well_rhs, well_inverse,
):
    gx, gy = lax.axis_size("gx"), lax.axis_size("gy")
    ix, iy = lax.axis_index("gx"), lax.axis_index("gy")
    phases, rows, cols, layers = adjoint_init.shape
    cells = rows * cols
    perfs = perf_well.shape[0]
    well_dev = well_rhs.shape[1]
    width = gy * well_dev // LANES
    unk = WELL_UNK * width
    base = PHASES * rows
    both = ("gx", "gy")
    flags = jnp.stack(
        [
            ix % 2,
            iy % 2,
            jnp.where(ix % 2 == 1, ix < gx - 1, ix > 0).astype(jnp.int32),
            jnp.where(iy % 2 == 1, iy < gy - 1, iy > 0).astype(jnp.int32),
        ]
    ).astype(jnp.int32)
    x = adjoint_init.reshape(phases, cells, layers)
    rhs = adjoint_rhs.reshape(phases, cells, layers)
    diag = cell_diag.reshape(phases, cells, layers)
    own_wells = jnp.concatenate([well_rhs, well_inverse.reshape(-1, well_dev)], axis=0)
    place = jnp.arange(gy * well_dev, dtype=jnp.int32) // well_dev == iy
    wide = jnp.where(place[None, :], jnp.tile(own_wells, (1, gy)), 0.0)
    wide = wide.reshape(5, WELL_UNK, width, LANES)
    wconst = jnp.transpose(wide, (2, 0, 1, 3))
    wconst = jnp.concatenate(
        [wconst[:, 0].reshape(unk, LANES), wconst[:, 1:].reshape(4 * unk, LANES)], axis=0
    )
    well_index = perf_owner[:, 0] * well_dev + perf_well

    full = base + unk
    first = pl.pallas_call(
        first_kernel,
        out_shape=(
            shape(phases, cells, layers),
            shape(2, 3, 3, rows, LANES),
            shape(perfs, 2 * cells, dtype=BF16),
            shape(cells, 2 * perfs, dtype=BF16),
            shape(width, perfs, LANES),
            shape(WELL_UNK, PHASES, perfs, LANES, dtype=BF16),
            shape(WELL_UNK, PHASES, perfs, LANES, dtype=BF16),
            shape(full + 5 * unk, LANES),
            shape(base, LANES),
            shape(PHASES * cols, LANES),
            shape(PHASES * cols, LANES),
        ),
        in_specs=[SM] + [VM] * 9,
        out_specs=(VM,) * 11,
        scratch_shapes=[
            pltpu.VMEM((2 * cells, PHASES * LANES), BF16),
            pltpu.VMEM((perfs, PHASES * LANES), F32),
        ],
        compiler_params=PARAMS,
        name="first",
    )
    inv, col_edges, pick, spread, well_hot, wc, cc, m1, m2_halo, m3, m4 = first(
        flags, x, jacobian, diag, perf_block.reshape(1, perfs), perf_block.reshape(perfs, 1),
        well_index.reshape(perfs, 1), well_coupling, cell_coupling, wconst,
    )

    def add(kept, own, got):
        return pl.pallas_call(
            functools.partial(add_kernel, base),
            out_shape=shape(*own.shape),
            in_specs=[VM] * 3,
            out_specs=VM,
            compiler_params=PARAMS,
            name="add",
        )(kept, own, got)

    inner = pl.pallas_call(
        inner_kernel,
        out_shape=shape(phases, cells, layers),
        in_specs=[VM] * 3,
        out_specs=VM,
        compiler_params=PARAMS,
        name="inner",
    )
    work = [
        pltpu.VMEM((2 * perfs, PHASES * LANES), BF16),
        pltpu.VMEM((cells, PHASES * LANES), F32),
    ]
    for sweep in range(ITERS):
        last = sweep == ITERS - 1
        g1 = lax.ppermute(m1, "gy", gy_swap(gy, 0))
        g3 = lax.ppermute(m3, both, gx_swap(gx, gy, 0))
        g4 = lax.ppermute(m4, both, gx_swap(gx, gy, 1))
        own = add(m2_halo, m1, g1)
        g2 = lax.ppermute(own, "gy", gy_swap(gy, 1))
        hop = 4
        while hop < gy:
            own = jnp.concatenate([own[:base], own[base:] + g2[base:]], axis=0)
            far = lax.ppermute(own[base:], "gy", [(j, (j + hop) % gy) for j in range(gy)])
            g2 = jnp.concatenate([g2[:base], far], axis=0)
            hop *= 2
        if sweep == 0:
            wconst = own[full:] + g2[full:]
            own, g1, g2 = own[:full], g1[:full], g2[:full]
        z = inner(x, jacobian, rhs)
        operands = (flags, z, own, g1, g2, g3, g4, wconst, inv, spread, well_hot, cc)
        if last:
            x, adj = pl.pallas_call(
                functools.partial(update_kernel, True),
                out_shape=(shape(phases, cells, layers), shape(width, WELL_UNK, LANES)),
                in_specs=[SM] + [VM] * 11,
                out_specs=(VM, VM),
                scratch_shapes=work,
                compiler_params=PARAMS,
                name="update_last",
            )(*operands)
        else:
            x, m1, m2_halo, m3, m4 = pl.pallas_call(
                functools.partial(update_kernel, False),
                out_shape=(
                    shape(phases, cells, layers),
                    shape(full, LANES),
                    shape(base, LANES),
                    shape(PHASES * cols, LANES),
                    shape(PHASES * cols, LANES),
                ),
                in_specs=[SM] + [VM] * 15,
                out_specs=(VM,) * 5,
                scratch_shapes=work
                + [
                    pltpu.VMEM((2 * cells, PHASES * LANES), BF16),
                    pltpu.VMEM((perfs, PHASES * LANES), F32),
                ],
                compiler_params=PARAMS,
                name="update",
            )(*operands, jacobian, col_edges, pick, wc)
    adj = jnp.transpose(adj, (1, 0, 2)).reshape(WELL_UNK, width * LANES)
    own_adj = lax.dynamic_slice_in_dim(adj, iy * well_dev, well_dev, axis=1)
    return x.reshape(adjoint_init.shape), own_adj


def solution(mesh):
    in_specs = (
        P(None, "gx", "gy", None),
        P(None, "gx", "gy", None),
        P(None, None, None, "gx", "gy", None),
        P(None, "gx", "gy", None),
        P(("gx", "gy"), None),
        P(("gx", "gy")),
        P(("gx", "gy")),
        P(None, None, ("gx", "gy")),
        P(None, None, ("gx", "gy")),
        P(None, ("gx", "gy")),
        P(None, None, ("gx", "gy")),
    )
    out_specs = (P(None, "gx", "gy", None), P(None, ("gx", "gy")))
    return jax.shard_map(body, mesh=mesh, in_specs=in_specs, out_specs=out_specs, check_vma=False)
```

```python
import functools

import jax
import jax.numpy as jnp
from jax import lax
from jax.experimental import pallas as pl
from jax.experimental.pallas import tpu as pltpu
from jax.sharding import PartitionSpec as P

PHASES = 3
WELL_UNK = 4
BLOCK = 64
ITERS = 8
LANES = 128
F32 = jnp.float32
BF16 = jnp.bfloat16
VM = pl.BlockSpec(memory_space=pltpu.VMEM)
HB = pl.BlockSpec(memory_space=pltpu.MemorySpace.HBM)
SM = pl.BlockSpec(memory_space=pltpu.SMEM)
PARAMS = pltpu.CompilerParams(vmem_limit_bytes=16 * 1024 * 1024)


def split_2(value):
    high = value.astype(BF16)
    return high, (value - high.astype(F32)).astype(BF16)


def edge_messages(flags, x_ref, row_ref, col_ref, m1_ref, m2_ref, m3_ref, m4_ref):
    rows, cols = col_ref.shape[3], row_ref.shape[3]
    gx_odd, gy_odd = flags[0] == 1, flags[1] == 1
    x_first = [x_ref[r, 0:cols, :] for r in range(PHASES)]
    x_last = [x_ref[r, (rows - 1) * cols : rows * cols, :] for r in range(PHASES)]
    c_first = [x_ref[r, pl.ds(0, rows, stride=cols), :] for r in range(PHASES)]
    c_last = [x_ref[r, pl.ds(cols - 1, rows, stride=cols), :] for r in range(PHASES)]
    for t in range(PHASES):
        up = sum(row_ref[0, r, t] * x_first[r] for r in range(PHASES))
        down = sum(row_ref[1, r, t] * x_last[r] for r in range(PHASES))
        left = sum(col_ref[0, r, t] * c_first[r] for r in range(PHASES))
        right = sum(col_ref[1, r, t] * c_last[r] for r in range(PHASES))
        m3_ref[t * cols : (t + 1) * cols, :] = jnp.where(gx_odd, up, down)
        m4_ref[t * cols : (t + 1) * cols, :] = jnp.where(gx_odd, down, up)
        m1_ref[t * rows : (t + 1) * rows, :] = jnp.where(gy_odd, left, right)
        m2_ref[t * rows : (t + 1) * rows, :] = jnp.where(gy_odd, right, left)


def well_partials(x_ref, pick_ref, well_ref, wc_ref, xs_ref, g_ref, write):
    cells = x_ref.shape[1]
    perfs = pick_ref.shape[0]
    for r in range(PHASES):
        high, low = split_2(x_ref[r])
        xs_ref[0:cells, r * LANES : (r + 1) * LANES] = high
        xs_ref[cells : 2 * cells, r * LANES : (r + 1) * LANES] = low
    g_ref[...] = jnp.dot(pick_ref[...], xs_ref[...], preferred_element_type=F32)
    width = well_ref.shape[0]
    chunk = 64
    totals = [[jnp.zeros((8, LANES), F32) for _ in range(width)] for _ in range(WELL_UNK)]
    for start in range(0, perfs, chunk):
        rows = slice(start, start + chunk)
        picked = [g_ref[rows, r * LANES : (r + 1) * LANES] for r in range(PHASES)]
        for u in range(WELL_UNK):
            lane_terms = sum(wc_ref[u, r, rows].astype(F32) * picked[r] for r in range(PHASES))
            term = jnp.sum(lane_terms, axis=1, keepdims=True)
            for h in range(width):
                spread = well_ref[h, rows, :] * term
                totals[u][h] = totals[u][h] + sum(spread[i : i + 8] for i in range(0, chunk, 8))
    for h in range(width):
        for u in range(WELL_UNK):
            write(h * WELL_UNK + u, jnp.sum(totals[u][h], axis=0, keepdims=True))


def expanded(eye, coupling_ref, u, own_half, out_ref):
    for r in range(PHASES):
        piece = coupling_ref[u, r * BLOCK : (r + 1) * BLOCK, :]
        doubled = jnp.concatenate([piece, piece], axis=0)
        out_ref[u, r] = jnp.where(own_half, turned(eye, doubled), 0.0).astype(BF16)


def turned(eye, value):
    return lax.dot_general(eye, value, (((1,), (1,)), ((), ())), preferred_element_type=F32)


def hot(mask):
    return mask.astype(F32).astype(BF16)


def iota(dims, axis):
    return lax.broadcasted_iota(jnp.int32, dims, axis)


def first_kernel(
    flags, x_in, jac_in, rhs_in, diag_in, wcoef_in, ccoef_in,
    block_in, well_in, owner_in, rhs_well_in, inv_well_in,
    x_ref, jac_ref, rhs_ref, inv_ref, row_ref, col_ref, pick_ref, spread_ref, well_ref, wc_ref,
    cc_ref, m1_ref, m2_ref, m3_ref, m4_ref, wcoef, ccoef, xs_ref, g_ref,
    block_row, well_row, owner_row, rhs_well, inv_well, sems, small_sems,
):
    pairs = [
        (block_in, block_row), (well_in, well_row), (owner_in, owner_row),
        (rhs_well_in, rhs_well), (inv_well_in, inv_well),
    ]
    small = [pltpu.make_async_copy(a, b, small_sems.at[i]) for i, (a, b) in enumerate(pairs)]
    for copy in small:
        copy.start()
    pairs = [
        (wcoef_in, wcoef), (ccoef_in, ccoef), (x_in, x_ref),
        (jac_in, jac_ref), (diag_in, inv_ref), (rhs_in, rhs_ref),
    ]
    copies = [pltpu.make_async_copy(a, b, sems.at[i]) for i, (a, b) in enumerate(pairs)]
    for copy in copies:
        copy.start()
    rows, cols = jac_ref.shape[3], jac_ref.shape[4]
    cells = rows * cols
    perfs = block_row.shape[1]
    width = well_ref.shape[0]
    well_dev = rhs_well.shape[1]
    base, unk = PHASES * rows, WELL_UNK * width
    eye = hot(iota((perfs, perfs), 0) == iota((perfs, perfs), 1))
    for copy in small:
        copy.wait()
    block = block_row[...]
    spread = hot(iota((cells, perfs), 0) == block // 2)
    spread_ref[:, 0:perfs] = spread
    spread_ref[:, perfs : 2 * perfs] = spread
    pick = turned(eye, spread).astype(BF16)
    pick_ref[:, 0:cells] = pick
    pick_ref[:, cells : 2 * cells] = pick
    own_half = turned(eye, hot(iota((LANES, perfs), 0) // BLOCK == block % 2)) > 0.5
    for h in range(width):
        slot = iota((LANES, perfs), 0) + h * LANES
        well = owner_row[...] * well_dev + well_row[...]
        well_ref[h] = turned(eye, hot(slot == well))
        place = iota((well_dev, LANES), 0) + flags[4] * well_dev
        place = (place == iota((well_dev, LANES), 1) + h * LANES).astype(F32)
        for v in range(WELL_UNK + 1):
            value = rhs_well[...] if v == 0 else inv_well[v - 1]
            value = jnp.dot(
                value, place, precision=lax.Precision.HIGHEST, preferred_element_type=F32
            )
            at = base + unk
            at += h * WELL_UNK if v == 0 else unk + (h * WELL_UNK + v - 1) * WELL_UNK
            m1_ref[at : at + WELL_UNK, :] = value
    copies[0].wait()
    for u in range(WELL_UNK):
        expanded(eye, wcoef, u, own_half, wc_ref)
    copies[1].wait()
    for u in range(WELL_UNK):
        expanded(eye, ccoef, u, own_half, cc_ref)
    copies[2].wait()

    def write(row, value):
        m1_ref[base + row : base + row + 1, :] = value

    well_partials(x_ref, pick_ref, well_ref, wc_ref, xs_ref, g_ref, write)
    copies[3].wait()
    for r in range(PHASES):
        for t in range(PHASES):
            row_ref[0, r, t] = jac_ref[1, r, t, 0].astype(F32)
            row_ref[1, r, t] = jac_ref[2, r, t, rows - 1].astype(F32)
            for i in range(rows):
                col_ref[0, r, t, i : i + 1, :] = jac_ref[3, r, t, i, 0:8].astype(F32)[0:1]
                edge = jac_ref[4, r, t, i, cols - 8 : cols].astype(F32)
                col_ref[1, r, t, i : i + 1, :] = edge[7:8]
    edge_messages(flags, x_ref, row_ref, col_ref, m1_ref, m2_ref, m3_ref, m4_ref)
    copies[4].wait()
    inv_ref[...] = 1.0 / inv_ref[...]
    copies[5].wait()


def add_kernel(base, kept_ref, own_ref, got_ref, out_ref):
    out_ref[0:base, :] = kept_ref[...]
    out_ref[base:, :] = own_ref[base:, :] + got_ref[base:, :]


def inner_kernel(widen, x_ref, jac_ref, rhs_ref, z_ref, *rest):
    rows, cols = jac_ref.shape[3], jac_ref.shape[4]
    lane, col = iota((cols, LANES), 1), iota((cols, LANES), 0)

    def row_body(i, carry):
        before = jnp.where(i == 0, rows - 1, i - 1)
        after = jnp.where(i == rows - 1, 0, i + 1)
        open_row = {1: (after > 0).astype(F32), 2: (before < rows - 1).astype(F32)}
        shut_cell = {
            3: col == 0, 4: col == cols - 1, 5: lane == 0, 6: lane == LANES - 1
        }

        def load(row):
            start = pl.multiple_of(row * cols, cols)
            return [x_ref[r, pl.ds(start, cols), :] for r in range(PHASES)]

        def coefficient(d, r, t, row):
            if not widen:
                return jac_ref[d, r, t, row]
            value = jac_ref[d, r, t, row].astype(F32)
            if d in open_row:
                value = value * open_row[d]
            if d in shut_cell:
                value = jnp.where(shut_cell[d], 0.0, value)
            rest[0][d, r, t, row] = value
            return value

        def term(d, t, row, values):
            return sum(coefficient(d, r, t, row) * values[r] for r in range(PHASES))

        here, values_before, values_after = load(i), load(before), load(after)
        start = pl.multiple_of(i * cols, cols)
        for t in range(PHASES):
            total = term(0, t, i, here)
            total = total + term(1, t, after, values_after)
            total = total + term(2, t, before, values_before)
            total = total + pltpu.roll(term(3, t, i, here), cols - 1, 0)
            total = total + pltpu.roll(term(4, t, i, here), 1, 0)
            total = total + pltpu.roll(term(5, t, i, here), LANES - 1, 1)
            total = total + pltpu.roll(term(6, t, i, here), 1, 1)
            z_ref[t, pl.ds(start, cols), :] = rhs_ref[t, pl.ds(start, cols), :] - total
        return carry

    lax.fori_loop(0, rows, row_body, 0)


def update_kernel(
    last, flags, z_ref, own, g1, g2, g3, g4, wconst, inv_ref, spread_ref, well_ref, cc_ref,
    *rest,
):
    if last:
        x_out, adj_ref, rs_ref, c_ref, x_ref, sems = rest
    else:
        (row_ref, col_ref, pick_ref, wc_ref, x_ref, m1_ref, m2_ref, m3_ref, m4_ref,
         rs_ref, c_ref, xs_ref, g_ref) = rest
    cells, perfs = spread_ref.shape[0], spread_ref.shape[1] // 2
    rows = (own.shape[0] - WELL_UNK * well_ref.shape[0]) // PHASES
    cols = cells // rows
    base = PHASES * rows
    width = well_ref.shape[0]
    unk = WELL_UNK * width
    terms = own[base : base + unk, :] + g2[base : base + unk, :]
    left = wconst[0:unk, :] - terms
    solved = []
    for h in range(width):
        value = 0.0
        for v in range(WELL_UNK):
            at = unk + (h * WELL_UNK + v) * WELL_UNK
            at_v = h * WELL_UNK + v
            value = value + wconst[at : at + WELL_UNK, :] * left[at_v : at_v + 1, :]
        solved.append(value)
    if last:
        well_dev = adj_ref.shape[1]
        mine = 0.0
        for h in range(width):
            place = iota((LANES, well_dev), 1) + flags[4] * well_dev
            place = (place == iota((LANES, well_dev), 0) + h * LANES).astype(F32)
            mine = mine + jnp.dot(
                solved[h], place, precision=lax.Precision.HIGHEST, preferred_element_type=F32
            )
        adj_ref[...] = mine
    chunk = 64
    for start in range(0, perfs, chunk):
        part = slice(start, start + chunk)
        value = [0.0] * PHASES
        for u in range(WELL_UNK):
            chosen = sum(well_ref[h, part, :] * solved[h][u : u + 1, :] for h in range(width))
            factor = jnp.sum(chosen, axis=1, keepdims=True)
            for r in range(PHASES):
                value[r] = value[r] + cc_ref[u, r, part].astype(F32) * factor
        for r in range(PHASES):
            high, low = split_2(value[r])
            rs_ref[start : start + chunk, r * LANES : (r + 1) * LANES] = high
            rs_ref[perfs + start : perfs + start + chunk, r * LANES : (r + 1) * LANES] = low
    c_ref[...] = jnp.dot(spread_ref[...], rs_ref[...], preferred_element_type=F32)
    gx_odd, gy_odd = flags[0] == 1, flags[1] == 1
    gx_open, gy_open = flags[2].astype(F32), flags[3].astype(F32)
    for t in range(PHASES):
        x_ref[t] = (z_ref[t] - c_ref[:, t * LANES : (t + 1) * LANES]) * inv_ref[t]
    copies = []
    for t in range(PHASES):
        near, far = g3[t * cols : (t + 1) * cols, :], g4[t * cols : (t + 1) * cols, :] * gx_open
        first, final = slice(0, cols), slice((rows - 1) * cols, rows * cols)
        x_ref[t, first, :] = x_ref[t, first, :] - inv_ref[t, first, :] * jnp.where(gx_odd, near, far)
        x_ref[t, final, :] = x_ref[t, final, :] - inv_ref[t, final, :] * jnp.where(gx_odd, far, near)
        near, far = g1[t * rows : (t + 1) * rows, :], g2[t * rows : (t + 1) * rows, :] * gy_open
        first, final = pl.ds(0, rows, stride=cols), pl.ds(cols - 1, rows, stride=cols)
        x_ref[t, first, :] = x_ref[t, first, :] - inv_ref[t, first, :] * jnp.where(gy_odd, near, far)
        x_ref[t, final, :] = x_ref[t, final, :] - inv_ref[t, final, :] * jnp.where(gy_odd, far, near)
        if last:
            copies.append(pltpu.make_async_copy(x_ref.at[t], x_out.at[t], sems.at[t]))
            copies[t].start()
    for copy in copies:
        copy.wait()
    if not last:
        edge_messages(flags, x_ref, row_ref, col_ref, m1_ref, m2_ref, m3_ref, m4_ref)

        def write(row, value):
            m1_ref[base + row : base + row + 1, :] = value

        well_partials(x_ref, pick_ref, well_ref, wc_ref, xs_ref, g_ref, write)


def gx_swap(gx, gy, parity):
    pairs = []
    for i in range(gx):
        k = i ^ 1 if parity == 0 else ((i + 1) ^ 1) - 1
        for j in range(gy):
            pairs.append((i * gy + j, k * gy + j if 0 <= k < gx else i * gy + (j ^ 1)))
    return pairs


def gy_swap(gy, parity):
    if parity == 0:
        return [(j, j ^ 1) for j in range(gy)]
    return [(j, (((j + 1) ^ 1) - 1) % gy) for j in range(gy)]


def in_hbm(value):
    return pltpu.with_memory_space_constraint(value, pltpu.MemorySpace.HBM)


def shape(*dims, dtype=F32):
    return jax.ShapeDtypeStruct(dims, dtype)


def body(
    adjoint_init, adjoint_rhs, jacobian, cell_diag, perf_owner, perf_well, perf_block,
    well_coupling, cell_coupling, well_rhs, well_inverse,
):
    gx, gy = lax.axis_size("gx"), lax.axis_size("gy")
    ix, iy = lax.axis_index("gx"), lax.axis_index("gy")
    phases, rows, cols, layers = adjoint_init.shape
    cells = rows * cols
    perfs = perf_well.shape[0]
    well_dev = well_rhs.shape[1]
    width = gy * well_dev // LANES
    unk = WELL_UNK * width
    base = PHASES * rows
    both = ("gx", "gy")
    flags = jnp.stack(
        [
            ix % 2,
            iy % 2,
            jnp.where(ix % 2 == 1, ix < gx - 1, ix > 0).astype(jnp.int32),
            jnp.where(iy % 2 == 1, iy < gy - 1, iy > 0).astype(jnp.int32),
            iy,
        ]
    ).astype(jnp.int32)
    x = adjoint_init.reshape(phases, cells, layers)
    rhs = adjoint_rhs.reshape(phases, cells, layers)
    diag = cell_diag.reshape(phases, cells, layers)
    full = base + unk
    grid = shape(phases, cells, layers)
    jac_shape = shape(*jacobian.shape, dtype=BF16)
    first = pl.pallas_call(
        first_kernel,
        out_shape=(
            grid,
            jac_shape,
            grid,
            grid,
            shape(2, PHASES, PHASES, cols, LANES),
            shape(2, PHASES, PHASES, rows, LANES),
            shape(perfs, 2 * cells, dtype=BF16),
            shape(cells, 2 * perfs, dtype=BF16),
            shape(width, perfs, LANES),
            shape(WELL_UNK, PHASES, perfs, LANES, dtype=BF16),
            shape(WELL_UNK, PHASES, perfs, LANES, dtype=BF16),
            shape(full + 5 * unk, LANES),
            shape(base, LANES),
            shape(PHASES * cols, LANES),
            shape(PHASES * cols, LANES),
        ),
        in_specs=[SM] + [HB] * 11,
        out_specs=(VM,) * 15,
        scratch_shapes=[
            pltpu.VMEM(well_coupling.shape, BF16),
            pltpu.VMEM(cell_coupling.shape, BF16),
            pltpu.VMEM((2 * cells, PHASES * LANES), BF16),
            pltpu.VMEM((perfs, PHASES * LANES), F32),
            pltpu.VMEM((1, perfs), jnp.int32),
            pltpu.VMEM((1, perfs), jnp.int32),
            pltpu.VMEM((1, perfs), jnp.int32),
            pltpu.VMEM(well_rhs.shape, F32),
            pltpu.VMEM(well_inverse.shape, F32),
            pltpu.SemaphoreType.DMA((6,)),
            pltpu.SemaphoreType.DMA((5,)),
        ],
        compiler_params=PARAMS,
        name="first",
    )
    (x, jac, rhs, inv, row_edges, col_edges, pick, spread, well_hot, wc, cc, m1, m2_halo, m3,
     m4) = first(
        flags,
        *[
            in_hbm(v)
            for v in (
                x, jacobian, rhs, diag, well_coupling, cell_coupling,
                perf_block.reshape(1, perfs), perf_well.reshape(1, perfs),
                perf_owner.reshape(1, perfs), well_rhs, well_inverse,
            )
        ],
    )

    def add(kept, own, got):
        return pl.pallas_call(
            functools.partial(add_kernel, base),
            out_shape=shape(*own.shape),
            in_specs=[VM] * 3,
            out_specs=VM,
            compiler_params=PARAMS,
            name="add",
        )(kept, own, got)

    def inner(x, jac, rhs, widen):
        wide = (shape(*jac.shape),) if widen else ()
        return pl.pallas_call(
            functools.partial(inner_kernel, widen),
            out_shape=(grid,) + wide,
            in_specs=[VM] * 3,
            out_specs=(VM,) * (1 + len(wide)),
            compiler_params=PARAMS,
            name="inner_widen" if widen else "inner",
        )(x, jac, rhs)

    work = [
        pltpu.VMEM((2 * perfs, PHASES * LANES), BF16),
        pltpu.VMEM((cells, PHASES * LANES), F32),
    ]
    for sweep in range(ITERS):
        last = sweep == ITERS - 1
        g1 = lax.ppermute(m1, "gy", gy_swap(gy, 0))
        g3 = lax.ppermute(m3, both, gx_swap(gx, gy, 0))
        g4 = lax.ppermute(m4, both, gx_swap(gx, gy, 1))
        own = add(m2_halo, m1, g1)
        g2 = lax.ppermute(own, "gy", gy_swap(gy, 1))
        hop = 4
        while hop < gy:
            own = jnp.concatenate([own[:base], own[base:] + g2[base:]], axis=0)
            far = lax.ppermute(own[base:], "gy", [(j, (j + hop) % gy) for j in range(gy)])
            g2 = jnp.concatenate([g2[:base], far], axis=0)
            hop *= 2
        if sweep == 0:
            wconst = own[full:] + g2[full:]
            own, g1, g2 = own[:full], g1[:full], g2[:full]
        if sweep == 0:
            z, jac = inner(x, jac, rhs, True)
        else:
            (z,) = inner(x, jac, rhs, False)
        operands = (flags, z, own, g1, g2, g3, g4, wconst, inv, spread, well_hot, cc)
        if last:
            x, adj = pl.pallas_call(
                functools.partial(update_kernel, True),
                out_shape=(grid, shape(*well_rhs.shape)),
                in_specs=[SM] + [VM] * 11,
                out_specs=(HB, VM),
                scratch_shapes=work
                + [
                    pltpu.VMEM((phases, cells, layers), F32),
                    pltpu.SemaphoreType.DMA((PHASES,)),
                ],
                compiler_params=PARAMS,
                name="update_last",
            )(*operands)
        else:
            x, m1, m2_halo, m3, m4 = pl.pallas_call(
                functools.partial(update_kernel, False),
                out_shape=(
                    shape(phases, cells, layers),
                    shape(full, LANES),
                    shape(base, LANES),
                    shape(PHASES * cols, LANES),
                    shape(PHASES * cols, LANES),
                ),
                in_specs=[SM] + [VM] * 15,
                out_specs=(VM,) * 5,
                scratch_shapes=work
                + [
                    pltpu.VMEM((2 * cells, PHASES * LANES), BF16),
                    pltpu.VMEM((perfs, PHASES * LANES), F32),
                ],
                compiler_params=PARAMS,
                name="update",
            )(*operands, row_edges, col_edges, pick, wc)
    return x.reshape(adjoint_init.shape), adj


def solution(mesh):
    in_specs = (
        P(None, "gx", "gy", None),
        P(None, "gx", "gy", None),
        P(None, None, None, "gx", "gy", None),
        P(None, "gx", "gy", None),
        P(("gx", "gy"), None),
        P(("gx", "gy")),
        P(("gx", "gy")),
        P(None, None, ("gx", "gy")),
        P(None, None, ("gx", "gy")),
        P(None, ("gx", "gy")),
        P(None, None, ("gx", "gy")),
    )
    out_specs = (P(None, "gx", "gy", None), P(None, ("gx", "gy")))
    return jax.shard_map(body, mesh=mesh, in_specs=in_specs, out_specs=out_specs, check_vma=False)
```

```python
import functools

import jax
import jax.numpy as jnp
from jax import lax
from jax.experimental import pallas as pl
from jax.experimental.pallas import tpu as pltpu
from jax.sharding import PartitionSpec as P

PHASES = 3
WELL_UNK = 4
BLOCK = 64
ITERS = 8
LANES = 128
F32 = jnp.float32
BF16 = jnp.bfloat16
VM = pl.BlockSpec(memory_space=pltpu.VMEM)
HB = pl.BlockSpec(memory_space=pltpu.MemorySpace.HBM)
SM = pl.BlockSpec(memory_space=pltpu.SMEM)
PARAMS = pltpu.CompilerParams(vmem_limit_bytes=16 * 1024 * 1024)


def split_2(value):
    high = value.astype(BF16)
    return high, (value - high.astype(F32)).astype(BF16)


def edge_messages(flags, x_ref, row_ref, col_ref, m1_ref, m2_ref, m3_ref, m4_ref):
    rows, cols = col_ref.shape[3], row_ref.shape[3]
    gx_odd, gy_odd = flags[0] == 1, flags[1] == 1
    x_first = [x_ref[r, 0:cols, :] for r in range(PHASES)]
    x_last = [x_ref[r, (rows - 1) * cols : rows * cols, :] for r in range(PHASES)]
    c_first = [x_ref[r, pl.ds(0, rows, stride=cols), :] for r in range(PHASES)]
    c_last = [x_ref[r, pl.ds(cols - 1, rows, stride=cols), :] for r in range(PHASES)]
    for t in range(PHASES):
        up = sum(row_ref[0, r, t] * x_first[r] for r in range(PHASES))
        down = sum(row_ref[1, r, t] * x_last[r] for r in range(PHASES))
        left = sum(col_ref[0, r, t] * c_first[r] for r in range(PHASES))
        right = sum(col_ref[1, r, t] * c_last[r] for r in range(PHASES))
        m3_ref[t * cols : (t + 1) * cols, :] = jnp.where(gx_odd, up, down)
        m4_ref[t * cols : (t + 1) * cols, :] = jnp.where(gx_odd, down, up)
        m1_ref[t * rows : (t + 1) * rows, :] = jnp.where(gy_odd, left, right)
        m2_ref[t * rows : (t + 1) * rows, :] = jnp.where(gy_odd, right, left)


def picked_rows(r, x_ref, pick_ref, xs_ref, g_ref):
    high, low = split_2(x_ref[r])
    xs_ref[r, :, 0:LANES] = high
    xs_ref[r, :, LANES : 2 * LANES] = low
    both = jnp.dot(pick_ref[...], xs_ref[r], preferred_element_type=F32)
    g_ref[r] = both[:, 0:LANES] + both[:, LANES:]


def well_partials(pick_ref, well_ref, wc_ref, g_ref, write):
    perfs = pick_ref.shape[0]
    width = well_ref.shape[0]
    chunk = 64
    totals = [[jnp.zeros((8, LANES), F32) for _ in range(width)] for _ in range(WELL_UNK)]
    for start in range(0, perfs, chunk):
        rows = slice(start, start + chunk)
        picked = [g_ref[r, rows, :] for r in range(PHASES)]
        for u in range(WELL_UNK):
            lane_terms = sum(wc_ref[u, r, rows].astype(F32) * picked[r] for r in range(PHASES))
            term = jnp.sum(lane_terms, axis=1, keepdims=True)
            for h in range(width):
                spread = well_ref[h, rows, :] * term
                totals[u][h] = totals[u][h] + sum(spread[i : i + 8] for i in range(0, chunk, 8))
    for h in range(width):
        for u in range(WELL_UNK):
            write(h * WELL_UNK + u, jnp.sum(totals[u][h], axis=0, keepdims=True))


def expanded(eye, coupling_ref, u, own_half, out_ref):
    for r in range(PHASES):
        piece = coupling_ref[u, r * BLOCK : (r + 1) * BLOCK, :]
        doubled = jnp.concatenate([piece, piece], axis=0)
        out_ref[u, r] = jnp.where(own_half, turned(eye, doubled), 0.0).astype(BF16)


def turned(eye, value):
    return lax.dot_general(eye, value, (((1,), (1,)), ((), ())), preferred_element_type=F32)


def hot(mask):
    return mask.astype(F32).astype(BF16)


def iota(dims, axis):
    return lax.broadcasted_iota(jnp.int32, dims, axis)


def first_kernel(
    flags, x_in, jac_in, rhs_in, diag_in, wcoef_in, ccoef_in,
    block_in, well_in, owner_in, rhs_well_in, inv_well_in,
    x_ref, jac_ref, rhs_ref, inv_ref, row_ref, col_ref, pick_ref, spread_ref, well_ref, wc_ref,
    cc_ref, m1_ref, m2_ref, m3_ref, m4_ref, wcoef, ccoef, xs_ref, g_ref,
    block_row, well_row, owner_row, rhs_well, inv_well, row_raw, col_raw, held, sems, small_sems,
):
    rows, cols = jac_in.shape[3], jac_in.shape[4]
    early = rows // 4 + 2
    pairs = [
        (block_in, block_row), (well_in, well_row), (owner_in, owner_row),
        (rhs_well_in, rhs_well), (inv_well_in, inv_well),
    ]
    small = [pltpu.make_async_copy(a, b, small_sems.at[i]) for i, (a, b) in enumerate(pairs)]
    for copy in small:
        copy.start()
    pairs = [
        (wcoef_in, wcoef), (ccoef_in, ccoef), (x_in, x_ref),
        (jac_in.at[1, :, :, 0], row_raw.at[0]),
        (jac_in.at[2, :, :, rows - 1], row_raw.at[1]),
        (jac_in.at[3, :, :, :, 0:8], col_raw.at[0]),
        (jac_in.at[4, :, :, :, cols - 8 : cols], col_raw.at[1]),
        (diag_in, inv_ref),
        (jac_in.at[:, :, :, rows - 1], jac_ref.at[:, :, :, rows - 1]),
        (jac_in.at[:, :, :, 0:early], jac_ref.at[:, :, :, 0:early]), (rhs_in, rhs_ref),
    ]
    copies = [pltpu.make_async_copy(a, b, sems.at[i]) for i, (a, b) in enumerate(pairs)]
    for copy in copies:
        copy.start()
    cells = rows * cols
    perfs = block_row.shape[1]
    width = well_ref.shape[0]
    well_dev = rhs_well.shape[1]
    base, unk = PHASES * rows, WELL_UNK * width
    eye = hot(iota((perfs, perfs), 0) == iota((perfs, perfs), 1))
    for copy in small:
        copy.wait()
    block = block_row[...]
    spread = hot(iota((cells, perfs), 0) == block // 2)
    spread_ref[...] = spread
    pick = turned(eye, spread).astype(BF16)
    pick_ref[...] = pick
    own_half = turned(eye, hot(iota((LANES, perfs), 0) // BLOCK == block % 2)) > 0.5
    for h in range(width):
        slot = iota((LANES, perfs), 0) + h * LANES
        well = owner_row[...] * well_dev + well_row[...]
        well_ref[h] = turned(eye, hot(slot == well))
    held[...] = jnp.zeros_like(held)
    held[0:WELL_UNK, 0:well_dev] = rhs_well[...]
    for v in range(WELL_UNK):
        held[(v + 1) * WELL_UNK : (v + 2) * WELL_UNK, 0:well_dev] = inv_well[v]
    own_lane = flags[4] * well_dev
    placed = pltpu.roll(held[...], own_lane % LANES, 1)
    for h in range(width):
        value = jnp.where(own_lane // LANES == h, placed, 0.0)
        at = base + unk + h * WELL_UNK
        m1_ref[at : at + WELL_UNK, :] = value[0:WELL_UNK]
        at = base + 2 * unk + h * WELL_UNK * WELL_UNK
        m1_ref[at : at + WELL_UNK * WELL_UNK, :] = value[WELL_UNK : 5 * WELL_UNK]
    copies[0].wait()
    for u in range(WELL_UNK):
        expanded(eye, wcoef, u, own_half, wc_ref)
    copies[1].wait()
    for u in range(WELL_UNK):
        expanded(eye, ccoef, u, own_half, cc_ref)
    copies[2].wait()

    def write(row, value):
        m1_ref[base + row : base + row + 1, :] = value

    for r in range(PHASES):
        picked_rows(r, x_ref, pick_ref, xs_ref, g_ref)
    well_partials(pick_ref, well_ref, wc_ref, g_ref, write)
    for copy in copies[3:7]:
        copy.wait()
    row_ref[...] = row_raw[...].astype(F32)
    for r in range(PHASES):
        for t in range(PHASES):
            for i in range(rows):
                col_ref[0, r, t, i : i + 1, :] = col_raw[0, r, t, i].astype(F32)[0:1]
                col_ref[1, r, t, i : i + 1, :] = col_raw[1, r, t, i].astype(F32)[7:8]
    edge_messages(flags, x_ref, row_ref, col_ref, m1_ref, m2_ref, m3_ref, m4_ref)
    copies[7].wait()
    inv_ref[...] = 1.0 / inv_ref[...]
    for copy in copies[8:]:
        copy.wait()


def add_kernel(base, kept_ref, own_ref, got_ref, out_ref):
    out_ref[0:base, :] = kept_ref[...]
    out_ref[base:, :] = own_ref[base:, :] + got_ref[base:, :]


def inner_kernel(widen, x_ref, jac_in, rhs_ref, *rest):
    rows, cols = jac_in.shape[3], jac_in.shape[4]
    early = rows // 4 + 2
    z_ref = rest[1] if widen else rest[0]
    if widen:
        wide_ref, jac_ref, sems = rest[2:]

        def fetch(row):
            return pltpu.make_async_copy(
                jac_in.at[:, :, :, row], jac_ref.at[:, :, :, row], sems.at[row]
            )

        for row in range(early, rows - 1):
            fetch(row).start()
    else:
        jac_ref = jac_in
    lane, col = iota((cols, LANES), 1), iota((cols, LANES), 0)

    def row_body(i, carry):
        if widen:
            pl.when((i + 1 >= early) & (i < rows - 2))(lambda: fetch(i + 1).wait())
        before = jnp.where(i == 0, rows - 1, i - 1)
        after = jnp.where(i == rows - 1, 0, i + 1)
        open_row = {1: (after > 0).astype(F32), 2: (before < rows - 1).astype(F32)}
        shut_cell = {
            3: col == 0, 4: col == cols - 1, 5: lane == 0, 6: lane == LANES - 1
        }

        def load(row):
            start = pl.multiple_of(row * cols, cols)
            return [x_ref[r, pl.ds(start, cols), :] for r in range(PHASES)]

        def coefficient(d, r, t, row):
            if not widen:
                return jac_ref[d, r, t, row]
            value = jac_ref[d, r, t, row].astype(F32)
            if d in open_row:
                value = value * open_row[d]
            if d in shut_cell:
                value = jnp.where(shut_cell[d], 0.0, value)
            wide_ref[d, r, t, row] = value
            return value

        def term(d, t, row, values):
            return sum(coefficient(d, r, t, row) * values[r] for r in range(PHASES))

        here, values_before, values_after = load(i), load(before), load(after)
        start = pl.multiple_of(i * cols, cols)
        for t in range(PHASES):
            total = term(0, t, i, here)
            total = total + term(1, t, after, values_after)
            total = total + term(2, t, before, values_before)
            total = total + pltpu.roll(term(3, t, i, here), cols - 1, 0)
            total = total + pltpu.roll(term(4, t, i, here), 1, 0)
            total = total + pltpu.roll(term(5, t, i, here), LANES - 1, 1)
            total = total + pltpu.roll(term(6, t, i, here), 1, 1)
            z_ref[t, pl.ds(start, cols), :] = rhs_ref[t, pl.ds(start, cols), :] - total
        return carry

    lax.fori_loop(0, rows, row_body, 0, unroll=1 if widen else 2)


def update_kernel(
    last, flags, z_ref, own, g1, g2, g3, g4, wconst, inv_ref, spread_ref, well_ref, cc_ref,
    *rest,
):
    if last:
        x_out, adj_ref, rs_ref, x_ref, sems = rest
    else:
        (row_ref, col_ref, pick_ref, wc_ref, x_ref, m1_ref, m2_ref, m3_ref, m4_ref,
         rs_ref, xs_ref, g_ref) = rest
    cells, perfs = spread_ref.shape
    rows = (own.shape[0] - WELL_UNK * well_ref.shape[0]) // PHASES
    cols = cells // rows
    base = PHASES * rows
    width = well_ref.shape[0]
    unk = WELL_UNK * width
    terms = own[base : base + unk, :] + g2[base : base + unk, :]
    left = wconst[0:unk, :] - terms
    solved = []
    for h in range(width):
        value = 0.0
        for v in range(WELL_UNK):
            at = unk + (h * WELL_UNK + v) * WELL_UNK
            at_v = h * WELL_UNK + v
            value = value + wconst[at : at + WELL_UNK, :] * left[at_v : at_v + 1, :]
        solved.append(value)
    chunk = 64
    for start in range(0, perfs, chunk):
        part = slice(start, start + chunk)
        value = [0.0] * PHASES
        for u in range(WELL_UNK):
            chosen = sum(well_ref[h, part, :] * solved[h][u : u + 1, :] for h in range(width))
            factor = jnp.sum(chosen, axis=1, keepdims=True)
            for r in range(PHASES):
                value[r] = value[r] + cc_ref[u, r, part].astype(F32) * factor
        for r in range(PHASES):
            high, low = split_2(value[r])
            rs_ref[r, part, 0:LANES] = high
            rs_ref[r, part, LANES : 2 * LANES] = low
    gx_odd, gy_odd = flags[0] == 1, flags[1] == 1
    gx_open, gy_open = flags[2].astype(F32), flags[3].astype(F32)
    copies = []
    for t in range(PHASES):
        both = jnp.dot(spread_ref[...], rs_ref[t], preferred_element_type=F32)
        x_ref[t] = (z_ref[t] - both[:, 0:LANES] - both[:, LANES:]) * inv_ref[t]
        near, far = g3[t * cols : (t + 1) * cols, :], g4[t * cols : (t + 1) * cols, :] * gx_open
        first, final = slice(0, cols), slice((rows - 1) * cols, rows * cols)
        x_ref[t, first, :] = x_ref[t, first, :] - inv_ref[t, first, :] * jnp.where(gx_odd, near, far)
        x_ref[t, final, :] = x_ref[t, final, :] - inv_ref[t, final, :] * jnp.where(gx_odd, far, near)
        near, far = g1[t * rows : (t + 1) * rows, :], g2[t * rows : (t + 1) * rows, :] * gy_open
        first, final = pl.ds(0, rows, stride=cols), pl.ds(cols - 1, rows, stride=cols)
        x_ref[t, first, :] = x_ref[t, first, :] - inv_ref[t, first, :] * jnp.where(gy_odd, near, far)
        x_ref[t, final, :] = x_ref[t, final, :] - inv_ref[t, final, :] * jnp.where(gy_odd, far, near)
        if last:
            copies.append(pltpu.make_async_copy(x_ref.at[t], x_out.at[t], sems.at[t]))
            copies[t].start()
        else:
            picked_rows(t, x_ref, pick_ref, xs_ref, g_ref)
    if last:
        well_dev = adj_ref.shape[1]
        mine = 0.0
        for h in range(width):
            place = iota((LANES, well_dev), 1) + flags[4] * well_dev
            place = (place == iota((LANES, well_dev), 0) + h * LANES).astype(F32)
            mine = mine + jnp.dot(
                solved[h], place, precision=lax.Precision.HIGHEST, preferred_element_type=F32
            )
        adj_ref[...] = mine
    for copy in copies:
        copy.wait()
    if not last:
        edge_messages(flags, x_ref, row_ref, col_ref, m1_ref, m2_ref, m3_ref, m4_ref)

        def write(row, value):
            m1_ref[base + row : base + row + 1, :] = value

        well_partials(pick_ref, well_ref, wc_ref, g_ref, write)


def gx_swap(gx, gy, parity):
    pairs = []
    for i in range(gx):
        k = i ^ 1 if parity == 0 else ((i + 1) ^ 1) - 1
        for j in range(gy):
            pairs.append((i * gy + j, k * gy + j if 0 <= k < gx else i * gy + (j ^ 1)))
    return pairs


def gy_swap(gy, parity):
    if parity == 0:
        return [(j, j ^ 1) for j in range(gy)]
    return [(j, (((j + 1) ^ 1) - 1) % gy) for j in range(gy)]


def in_hbm(value):
    return pltpu.with_memory_space_constraint(value, pltpu.MemorySpace.HBM)


def shape(*dims, dtype=F32):
    return jax.ShapeDtypeStruct(dims, dtype)


def body(
    adjoint_init, adjoint_rhs, jacobian, cell_diag, perf_owner, perf_well, perf_block,
    well_coupling, cell_coupling, well_rhs, well_inverse,
):
    gx, gy = lax.axis_size("gx"), lax.axis_size("gy")
    ix, iy = lax.axis_index("gx"), lax.axis_index("gy")
    phases, rows, cols, layers = adjoint_init.shape
    cells = rows * cols
    perfs = perf_well.shape[0]
    well_dev = well_rhs.shape[1]
    width = gy * well_dev // LANES
    unk = WELL_UNK * width
    base = PHASES * rows
    both = ("gx", "gy")
    flags = jnp.stack(
        [
            ix % 2,
            iy % 2,
            jnp.where(ix % 2 == 1, ix < gx - 1, ix > 0).astype(jnp.int32),
            jnp.where(iy % 2 == 1, iy < gy - 1, iy > 0).astype(jnp.int32),
            iy,
        ]
    ).astype(jnp.int32)
    x = adjoint_init.reshape(phases, cells, layers)
    rhs = adjoint_rhs.reshape(phases, cells, layers)
    diag = cell_diag.reshape(phases, cells, layers)
    full = base + unk
    grid = shape(phases, cells, layers)
    first = pl.pallas_call(
        first_kernel,
        out_shape=(
            grid,
            shape(*jacobian.shape, dtype=BF16),
            grid,
            grid,
            shape(2, PHASES, PHASES, cols, LANES),
            shape(2, PHASES, PHASES, rows, LANES),
            shape(perfs, cells, dtype=BF16),
            shape(cells, perfs, dtype=BF16),
            shape(width, perfs, LANES),
            shape(WELL_UNK, PHASES, perfs, LANES, dtype=BF16),
            shape(WELL_UNK, PHASES, perfs, LANES, dtype=BF16),
            shape(full + 5 * unk, LANES),
            shape(base, LANES),
            shape(PHASES * cols, LANES),
            shape(PHASES * cols, LANES),
        ),
        in_specs=[SM] + [HB] * 11,
        out_specs=(VM,) * 15,
        scratch_shapes=[
            pltpu.VMEM(well_coupling.shape, BF16),
            pltpu.VMEM(cell_coupling.shape, BF16),
            pltpu.VMEM((PHASES, cells, 2 * LANES), BF16),
            pltpu.VMEM((PHASES, perfs, LANES), F32),
            pltpu.VMEM((1, perfs), jnp.int32),
            pltpu.VMEM((1, perfs), jnp.int32),
            pltpu.VMEM((1, perfs), jnp.int32),
            pltpu.VMEM(well_rhs.shape, F32),
            pltpu.VMEM(well_inverse.shape, F32),
            pltpu.VMEM((2, PHASES, PHASES, cols, LANES), BF16),
            pltpu.VMEM((2, PHASES, PHASES, rows, 8, LANES), BF16),
            pltpu.VMEM((24, LANES), F32),
            pltpu.SemaphoreType.DMA((11,)),
            pltpu.SemaphoreType.DMA((5,)),
        ],
        compiler_params=PARAMS,
        name="first",
    )
    (x, jac_part, rhs, inv, row_edges, col_edges, pick, spread, well_hot, wc, cc, m1, m2_halo, m3,
     m4) = first(
        flags,
        *[
            in_hbm(v)
            for v in (
                x, jacobian, rhs, diag, well_coupling, cell_coupling,
                perf_block.reshape(1, perfs), perf_well.reshape(1, perfs),
                perf_owner.reshape(1, perfs), well_rhs, well_inverse,
            )
        ],
    )

    def add(kept, own, got):
        return pl.pallas_call(
            functools.partial(add_kernel, base),
            out_shape=shape(*own.shape),
            in_specs=[VM] * 3,
            out_specs=VM,
            compiler_params=PARAMS,
            name="add",
        )(kept, own, got)

    def inner_first(x, jac, rhs, jac_part):
        return pl.pallas_call(
            functools.partial(inner_kernel, True),
            out_shape=(grid, shape(*jac.shape), shape(*jac.shape, dtype=BF16)),
            in_specs=[VM, HB, VM, VM],
            out_specs=(VM,) * 3,
            scratch_shapes=[pltpu.SemaphoreType.DMA((rows,))],
            input_output_aliases={3: 2},
            compiler_params=PARAMS,
            name="inner_widen",
        )(x, in_hbm(jac), rhs, jac_part)[:2]

    inner = pl.pallas_call(
        functools.partial(inner_kernel, False),
        out_shape=grid,
        in_specs=[VM] * 3,
        out_specs=VM,
        compiler_params=PARAMS,
        name="inner",
    )
    work = [
        pltpu.VMEM((PHASES, perfs, 2 * LANES), BF16),
    ]
    for sweep in range(ITERS):
        last = sweep == ITERS - 1
        g1 = lax.ppermute(m1, "gy", gy_swap(gy, 0))
        g3 = lax.ppermute(m3, both, gx_swap(gx, gy, 0))
        g4 = lax.ppermute(m4, both, gx_swap(gx, gy, 1))
        own = add(m2_halo, m1, g1)
        g2 = lax.ppermute(own, "gy", gy_swap(gy, 1))
        hop = 4
        while hop < gy:
            own = jnp.concatenate([own[:base], own[base:] + g2[base:]], axis=0)
            far = lax.ppermute(own[base:], "gy", [(j, (j + hop) % gy) for j in range(gy)])
            g2 = jnp.concatenate([g2[:base], far], axis=0)
            hop *= 2
        if sweep == 0:
            wconst = own[full:] + g2[full:]
            own, g1, g2 = own[:full], g1[:full], g2[:full]
        if sweep == 0:
            z, jac = inner_first(x, jacobian, rhs, jac_part)
        else:
            z = inner(x, jac, rhs)
        operands = (flags, z, own, g1, g2, g3, g4, wconst, inv, spread, well_hot, cc)
        if last:
            x, adj = pl.pallas_call(
                functools.partial(update_kernel, True),
                out_shape=(grid, shape(*well_rhs.shape)),
                in_specs=[SM] + [VM] * 11,
                out_specs=(HB, VM),
                scratch_shapes=work
                + [
                    pltpu.VMEM((phases, cells, layers), F32),
                    pltpu.SemaphoreType.DMA((PHASES,)),
                ],
                compiler_params=PARAMS,
                name="update_last",
            )(*operands)
        else:
            x, m1, m2_halo, m3, m4 = pl.pallas_call(
                functools.partial(update_kernel, False),
                out_shape=(
                    shape(phases, cells, layers),
                    shape(full, LANES),
                    shape(base, LANES),
                    shape(PHASES * cols, LANES),
                    shape(PHASES * cols, LANES),
                ),
                in_specs=[SM] + [VM] * 15,
                out_specs=(VM,) * 5,
                scratch_shapes=work
                + [
                    pltpu.VMEM((PHASES, cells, 2 * LANES), BF16),
                    pltpu.VMEM((PHASES, perfs, LANES), F32),
                ],
                compiler_params=PARAMS,
                name="update",
            )(*operands, row_edges, col_edges, pick, wc)
    return x.reshape(adjoint_init.shape), adj


def solution(mesh):
    in_specs = (
        P(None, "gx", "gy", None),
        P(None, "gx", "gy", None),
        P(None, None, None, "gx", "gy", None),
        P(None, "gx", "gy", None),
        P(("gx", "gy"), None),
        P(("gx", "gy")),
        P(("gx", "gy")),
        P(None, None, ("gx", "gy")),
        P(None, None, ("gx", "gy")),
        P(None, ("gx", "gy")),
        P(None, None, ("gx", "gy")),
    )
    out_specs = (P(None, "gx", "gy", None), P(None, ("gx", "gy")))
    return jax.shard_map(body, mesh=mesh, in_specs=in_specs, out_specs=out_specs, check_vma=False)
```

```python
import functools

import jax
import jax.numpy as jnp
from jax import lax
from jax.experimental import pallas as pl
from jax.experimental.pallas import tpu as pltpu
from jax.sharding import PartitionSpec as P

PHASES = 3
WELL_UNK = 4
BLOCK = 64
ITERS = 8
LANES = 128
F32 = jnp.float32
BF16 = jnp.bfloat16
VM = pl.BlockSpec(memory_space=pltpu.VMEM)
HB = pl.BlockSpec(memory_space=pltpu.MemorySpace.HBM)
SM = pl.BlockSpec(memory_space=pltpu.SMEM)
PARAMS = pltpu.CompilerParams(vmem_limit_bytes=16 * 1024 * 1024)


def split_2(value):
    high = value.astype(BF16)
    return high, (value - high.astype(F32)).astype(BF16)


def edge_messages(flags, x_ref, row_ref, col_ref, m1_ref, m2_ref, m3_ref, m4_ref):
    rows, cols = col_ref.shape[3], row_ref.shape[3]
    gx_odd, gy_odd = flags[0] == 1, flags[1] == 1
    x_first = [x_ref[r, 0:cols, :] for r in range(PHASES)]
    x_last = [x_ref[r, (rows - 1) * cols : rows * cols, :] for r in range(PHASES)]
    c_first = [x_ref[r, pl.ds(0, rows, stride=cols), :] for r in range(PHASES)]
    c_last = [x_ref[r, pl.ds(cols - 1, rows, stride=cols), :] for r in range(PHASES)]
    for t in range(PHASES):
        up = sum(row_ref[0, r, t] * x_first[r] for r in range(PHASES))
        down = sum(row_ref[1, r, t] * x_last[r] for r in range(PHASES))
        left = sum(col_ref[0, r, t] * c_first[r] for r in range(PHASES))
        right = sum(col_ref[1, r, t] * c_last[r] for r in range(PHASES))
        m3_ref[t * cols : (t + 1) * cols, :] = jnp.where(gx_odd, up, down)
        m4_ref[t * cols : (t + 1) * cols, :] = jnp.where(gx_odd, down, up)
        m1_ref[t * rows : (t + 1) * rows, :] = jnp.where(gy_odd, left, right)
        m2_ref[t * rows : (t + 1) * rows, :] = jnp.where(gy_odd, right, left)


def picked_rows(r, x_ref, pick_ref, xs_ref, g_ref):
    high, low = split_2(x_ref[r])
    xs_ref[r, :, 0:LANES] = high
    xs_ref[r, :, LANES : 2 * LANES] = low
    both = jnp.dot(pick_ref[...], xs_ref[r], preferred_element_type=F32)
    g_ref[r] = both[:, 0:LANES] + both[:, LANES:]


def well_partials(pick_ref, well_ref, wc_ref, g_ref, write):
    perfs = pick_ref.shape[0]
    width = well_ref.shape[0]
    chunk = 64
    totals = [[jnp.zeros((8, LANES), F32) for _ in range(width)] for _ in range(WELL_UNK)]
    for start in range(0, perfs, chunk):
        rows = slice(start, start + chunk)
        picked = [g_ref[r, rows, :] for r in range(PHASES)]
        for u in range(WELL_UNK):
            lane_terms = sum(wc_ref[u, r, rows].astype(F32) * picked[r] for r in range(PHASES))
            term = jnp.sum(lane_terms, axis=1, keepdims=True)
            for h in range(width):
                spread = well_ref[h, rows, :] * term
                totals[u][h] = totals[u][h] + sum(spread[i : i + 8] for i in range(0, chunk, 8))
    for h in range(width):
        for u in range(WELL_UNK):
            write(h * WELL_UNK + u, jnp.sum(totals[u][h], axis=0, keepdims=True))


def expanded(eye, coupling_ref, u, own_half, out_ref):
    for r in range(PHASES):
        piece = coupling_ref[u, r * BLOCK : (r + 1) * BLOCK, :]
        doubled = jnp.concatenate([piece, piece], axis=0)
        out_ref[u, r] = jnp.where(own_half, turned(eye, doubled), 0.0).astype(BF16)


def turned(eye, value):
    return lax.dot_general(eye, value, (((1,), (1,)), ((), ())), preferred_element_type=F32)


def hot(mask):
    return mask.astype(F32).astype(BF16)


def iota(dims, axis):
    return lax.broadcasted_iota(jnp.int32, dims, axis)


def first_kernel(
    flags, x_in, jac_in, rhs_in, wcoef_in,
    block_in, well_in, owner_in, rhs_well_in, inv_well_in,
    x_ref, jac_ref, rhs_ref, row_ref, col_ref, pick_ref, spread_ref, well_ref, wc_ref,
    half_ref, m1_ref, m2_ref, m3_ref, m4_ref, wcoef, xs_ref, g_ref,
    block_row, well_row, owner_row, rhs_well, inv_well, row_raw, col_raw, held, sems, small_sems,
):
    rows, cols = jac_in.shape[3], jac_in.shape[4]
    early = rows // 4 + 2
    pairs = [
        (block_in, block_row), (well_in, well_row), (owner_in, owner_row),
        (rhs_well_in, rhs_well), (inv_well_in, inv_well),
    ]
    small = [pltpu.make_async_copy(a, b, small_sems.at[i]) for i, (a, b) in enumerate(pairs)]
    for copy in small:
        copy.start()
    pairs = [
        (wcoef_in, wcoef), (x_in, x_ref),
        (jac_in.at[1, :, :, 0], row_raw.at[0]),
        (jac_in.at[2, :, :, rows - 1], row_raw.at[1]),
        (jac_in.at[3, :, :, :, 0:8], col_raw.at[0]),
        (jac_in.at[4, :, :, :, cols - 8 : cols], col_raw.at[1]),
        (jac_in.at[:, :, :, rows - 1], jac_ref.at[:, :, :, rows - 1]),
        (jac_in.at[:, :, :, 0:early], jac_ref.at[:, :, :, 0:early]), (rhs_in, rhs_ref),
    ]
    copies = [pltpu.make_async_copy(a, b, sems.at[i]) for i, (a, b) in enumerate(pairs)]
    for copy in copies:
        copy.start()
    cells = rows * cols
    perfs = block_row.shape[1]
    width = well_ref.shape[0]
    well_dev = rhs_well.shape[1]
    base, unk = PHASES * rows, WELL_UNK * width
    eye = hot(iota((perfs, perfs), 0) == iota((perfs, perfs), 1))
    for copy in small:
        copy.wait()
    block = block_row[...]
    spread = hot(iota((cells, perfs), 0) == block // 2)
    spread_ref[...] = spread
    pick = turned(eye, spread).astype(BF16)
    pick_ref[...] = pick
    half_ref[...] = turned(eye, hot(iota((LANES, perfs), 0) // BLOCK == block % 2))
    own_half = half_ref[...] > 0.5
    for h in range(width):
        slot = iota((LANES, perfs), 0) + h * LANES
        well = owner_row[...] * well_dev + well_row[...]
        well_ref[h] = turned(eye, hot(slot == well))
    held[...] = jnp.zeros_like(held)
    held[0:WELL_UNK, 0:well_dev] = rhs_well[...]
    for v in range(WELL_UNK):
        held[(v + 1) * WELL_UNK : (v + 2) * WELL_UNK, 0:well_dev] = inv_well[v]
    own_lane = flags[4] * well_dev
    placed = pltpu.roll(held[...], own_lane % LANES, 1)
    for h in range(width):
        value = jnp.where(own_lane // LANES == h, placed, 0.0)
        at = base + unk + h * WELL_UNK
        m1_ref[at : at + WELL_UNK, :] = value[0:WELL_UNK]
        at = base + 2 * unk + h * WELL_UNK * WELL_UNK
        m1_ref[at : at + WELL_UNK * WELL_UNK, :] = value[WELL_UNK : 5 * WELL_UNK]
    copies[0].wait()
    for u in range(WELL_UNK):
        expanded(eye, wcoef, u, own_half, wc_ref)
    copies[1].wait()

    def write(row, value):
        m1_ref[base + row : base + row + 1, :] = value

    for r in range(PHASES):
        picked_rows(r, x_ref, pick_ref, xs_ref, g_ref)
    well_partials(pick_ref, well_ref, wc_ref, g_ref, write)
    for copy in copies[2:6]:
        copy.wait()
    row_ref[...] = row_raw[...].astype(F32)
    for r in range(PHASES):
        for t in range(PHASES):
            for i in range(rows):
                col_ref[0, r, t, i : i + 1, :] = col_raw[0, r, t, i].astype(F32)[0:1]
                col_ref[1, r, t, i : i + 1, :] = col_raw[1, r, t, i].astype(F32)[7:8]
    edge_messages(flags, x_ref, row_ref, col_ref, m1_ref, m2_ref, m3_ref, m4_ref)
    for copy in copies[6:]:
        copy.wait()


def add_kernel(base, kept_ref, own_ref, got_ref, out_ref):
    out_ref[0:base, :] = kept_ref[...]
    out_ref[base:, :] = own_ref[base:, :] + got_ref[base:, :]


def inner_kernel(widen, x_ref, jac_in, rhs_ref, *rest):
    rows, cols = jac_in.shape[3], jac_in.shape[4]
    early = rows // 4 + 2
    z_ref = rest[0]
    if widen:
        ccoef_in, diag_in, half_ref, z_ref, wide_ref, jac_ref, cc_ref, inv_ref, ccoef, sems = rest[1:]

        def fetch(row):
            return pltpu.make_async_copy(
                jac_in.at[:, :, :, row], jac_ref.at[:, :, :, row], sems.at[row]
            )

        for row in range(early, rows - 1):
            fetch(row).start()
        extra = [
            pltpu.make_async_copy(ccoef_in, ccoef, sems.at[0]),
            pltpu.make_async_copy(diag_in, inv_ref, sems.at[1]),
        ]
        for copy in extra:
            copy.start()
    else:
        jac_ref = jac_in
    lane, col = iota((cols, LANES), 1), iota((cols, LANES), 0)

    def row_body(i, carry):
        if widen:
            pl.when((i + 1 >= early) & (i < rows - 2))(lambda: fetch(i + 1).wait())
        before = jnp.where(i == 0, rows - 1, i - 1)
        after = jnp.where(i == rows - 1, 0, i + 1)
        open_row = {1: (after > 0).astype(F32), 2: (before < rows - 1).astype(F32)}
        shut_cell = {
            3: col == 0, 4: col == cols - 1, 5: lane == 0, 6: lane == LANES - 1
        }

        def load(row):
            start = pl.multiple_of(row * cols, cols)
            return [x_ref[r, pl.ds(start, cols), :] for r in range(PHASES)]

        def coefficient(d, r, t, row):
            if not widen:
                return jac_ref[d, r, t, row]
            value = jac_ref[d, r, t, row].astype(F32)
            if d in open_row:
                value = value * open_row[d]
            if d in shut_cell:
                value = jnp.where(shut_cell[d], 0.0, value)
            wide_ref[d, r, t, row] = value
            return value

        def term(d, t, row, values):
            return sum(coefficient(d, r, t, row) * values[r] for r in range(PHASES))

        here, values_before, values_after = load(i), load(before), load(after)
        start = pl.multiple_of(i * cols, cols)
        for t in range(PHASES):
            total = term(0, t, i, here)
            total = total + term(1, t, after, values_after)
            total = total + term(2, t, before, values_before)
            total = total + pltpu.roll(term(3, t, i, here), cols - 1, 0)
            total = total + pltpu.roll(term(4, t, i, here), 1, 0)
            total = total + pltpu.roll(term(5, t, i, here), LANES - 1, 1)
            total = total + pltpu.roll(term(6, t, i, here), 1, 1)
            z_ref[t, pl.ds(start, cols), :] = rhs_ref[t, pl.ds(start, cols), :] - total
        return carry

    lax.fori_loop(0, rows, row_body, 0, unroll=1 if widen else 2)
    if widen:
        perfs = half_ref.shape[0]
        eye = hot(iota((perfs, perfs), 0) == iota((perfs, perfs), 1))
        for copy in extra:
            copy.wait()
        for u in range(WELL_UNK):
            expanded(eye, ccoef, u, half_ref[...] > 0.5, cc_ref)
        inv_ref[...] = 1.0 / inv_ref[...]


def update_kernel(
    last, flags, z_ref, own, g1, g2, g3, g4, wconst, inv_ref, spread_ref, well_ref, cc_ref,
    *rest,
):
    if last:
        x_out, adj_ref, rs_ref, x_ref, sems = rest
    else:
        (row_ref, col_ref, x_ref, m1_ref, m2_ref, m3_ref, m4_ref, rs_ref) = rest
    cells, perfs = spread_ref.shape
    rows = (own.shape[0] - WELL_UNK * well_ref.shape[0]) // PHASES
    cols = cells // rows
    base = PHASES * rows
    width = well_ref.shape[0]
    unk = WELL_UNK * width
    terms = own[base : base + unk, :] + g2[base : base + unk, :]
    left = wconst[0:unk, :] - terms
    solved = []
    for h in range(width):
        value = 0.0
        for v in range(WELL_UNK):
            at = unk + (h * WELL_UNK + v) * WELL_UNK
            at_v = h * WELL_UNK + v
            value = value + wconst[at : at + WELL_UNK, :] * left[at_v : at_v + 1, :]
        solved.append(value)
    chunk = 64
    for start in range(0, perfs, chunk):
        part = slice(start, start + chunk)
        value = [0.0] * PHASES
        for u in range(WELL_UNK):
            chosen = sum(well_ref[h, part, :] * solved[h][u : u + 1, :] for h in range(width))
            factor = jnp.sum(chosen, axis=1, keepdims=True)
            for r in range(PHASES):
                value[r] = value[r] + cc_ref[u, r, part].astype(F32) * factor
        for r in range(PHASES):
            high, low = split_2(value[r])
            rs_ref[r, part, 0:LANES] = high
            rs_ref[r, part, LANES : 2 * LANES] = low
    gx_odd, gy_odd = flags[0] == 1, flags[1] == 1
    gx_open, gy_open = flags[2].astype(F32), flags[3].astype(F32)
    copies = []
    for t in range(PHASES):
        both = jnp.dot(spread_ref[...], rs_ref[t], preferred_element_type=F32)
        x_ref[t] = (z_ref[t] - both[:, 0:LANES] - both[:, LANES:]) * inv_ref[t]
        near, far = g3[t * cols : (t + 1) * cols, :], g4[t * cols : (t + 1) * cols, :] * gx_open
        first, final = slice(0, cols), slice((rows - 1) * cols, rows * cols)
        x_ref[t, first, :] = x_ref[t, first, :] - inv_ref[t, first, :] * jnp.where(gx_odd, near, far)
        x_ref[t, final, :] = x_ref[t, final, :] - inv_ref[t, final, :] * jnp.where(gx_odd, far, near)
        near, far = g1[t * rows : (t + 1) * rows, :], g2[t * rows : (t + 1) * rows, :] * gy_open
        first, final = pl.ds(0, rows, stride=cols), pl.ds(cols - 1, rows, stride=cols)
        x_ref[t, first, :] = x_ref[t, first, :] - inv_ref[t, first, :] * jnp.where(gy_odd, near, far)
        x_ref[t, final, :] = x_ref[t, final, :] - inv_ref[t, final, :] * jnp.where(gy_odd, far, near)
        if last:
            copies.append(pltpu.make_async_copy(x_ref.at[t], x_out.at[t], sems.at[t]))
            copies[t].start()
    if last:
        well_dev = adj_ref.shape[1]
        mine = 0.0
        for h in range(width):
            place = iota((LANES, well_dev), 1) + flags[4] * well_dev
            place = (place == iota((LANES, well_dev), 0) + h * LANES).astype(F32)
            mine = mine + jnp.dot(
                solved[h], place, precision=lax.Precision.HIGHEST, preferred_element_type=F32
            )
        adj_ref[...] = mine
    for copy in copies:
        copy.wait()
    if not last:
        edge_messages(flags, x_ref, row_ref, col_ref, m1_ref, m2_ref, m3_ref, m4_ref)


def wells_kernel(
    x_ref, pick_ref, well_ref, wc_ref, halo_ref, pass_ref, m1_ref, passed_ref, xs_ref, g_ref
):
    base = halo_ref.shape[0]
    m1_ref[0:base, :] = halo_ref[...]
    passed_ref[...] = pass_ref[...]
    for t in range(PHASES):
        picked_rows(t, x_ref, pick_ref, xs_ref, g_ref)

    def write(row, value):
        m1_ref[base + row : base + row + 1, :] = value

    well_partials(pick_ref, well_ref, wc_ref, g_ref, write)


def gx_swap(gx, gy, parity):
    pairs = []
    for i in range(gx):
        k = i ^ 1 if parity == 0 else ((i + 1) ^ 1) - 1
        for j in range(gy):
            pairs.append((i * gy + j, k * gy + j if 0 <= k < gx else i * gy + (j ^ 1)))
    return pairs


def gy_swap(gy, parity):
    if parity == 0:
        return [(j, j ^ 1) for j in range(gy)]
    return [(j, (((j + 1) ^ 1) - 1) % gy) for j in range(gy)]


def in_hbm(value):
    return pltpu.with_memory_space_constraint(value, pltpu.MemorySpace.HBM)


def shape(*dims, dtype=F32):
    return jax.ShapeDtypeStruct(dims, dtype)


def body(
    adjoint_init, adjoint_rhs, jacobian, cell_diag, perf_owner, perf_well, perf_block,
    well_coupling, cell_coupling, well_rhs, well_inverse,
):
    gx, gy = lax.axis_size("gx"), lax.axis_size("gy")
    ix, iy = lax.axis_index("gx"), lax.axis_index("gy")
    phases, rows, cols, layers = adjoint_init.shape
    cells = rows * cols
    perfs = perf_well.shape[0]
    well_dev = well_rhs.shape[1]
    width = gy * well_dev // LANES
    unk = WELL_UNK * width
    base = PHASES * rows
    both = ("gx", "gy")
    flags = jnp.stack(
        [
            ix % 2,
            iy % 2,
            jnp.where(ix % 2 == 1, ix < gx - 1, ix > 0).astype(jnp.int32),
            jnp.where(iy % 2 == 1, iy < gy - 1, iy > 0).astype(jnp.int32),
            iy,
        ]
    ).astype(jnp.int32)
    x = adjoint_init.reshape(phases, cells, layers)
    rhs = adjoint_rhs.reshape(phases, cells, layers)
    diag = cell_diag.reshape(phases, cells, layers)
    full = base + unk
    grid = shape(phases, cells, layers)
    first = pl.pallas_call(
        first_kernel,
        out_shape=(
            grid,
            shape(*jacobian.shape, dtype=BF16),
            grid,
            shape(2, PHASES, PHASES, cols, LANES),
            shape(2, PHASES, PHASES, rows, LANES),
            shape(perfs, cells, dtype=BF16),
            shape(cells, perfs, dtype=BF16),
            shape(width, perfs, LANES),
            shape(WELL_UNK, PHASES, perfs, LANES, dtype=BF16),
            shape(perfs, LANES),
            shape(full + 5 * unk, LANES),
            shape(base, LANES),
            shape(PHASES * cols, LANES),
            shape(PHASES * cols, LANES),
        ),
        in_specs=[SM] + [HB] * 9,
        out_specs=(VM,) * 14,
        scratch_shapes=[
            pltpu.VMEM(well_coupling.shape, BF16),
            pltpu.VMEM((PHASES, cells, 2 * LANES), BF16),
            pltpu.VMEM((PHASES, perfs, LANES), F32),
            pltpu.VMEM((1, perfs), jnp.int32),
            pltpu.VMEM((1, perfs), jnp.int32),
            pltpu.VMEM((1, perfs), jnp.int32),
            pltpu.VMEM(well_rhs.shape, F32),
            pltpu.VMEM(well_inverse.shape, F32),
            pltpu.VMEM((2, PHASES, PHASES, cols, LANES), BF16),
            pltpu.VMEM((2, PHASES, PHASES, rows, 8, LANES), BF16),
            pltpu.VMEM((24, LANES), F32),
            pltpu.SemaphoreType.DMA((9,)),
            pltpu.SemaphoreType.DMA((5,)),
        ],
        compiler_params=PARAMS,
        name="first",
    )
    (x, jac_part, rhs, row_edges, col_edges, pick, spread, well_hot, wc, own_half, m1, m2_halo, m3,
     m4) = first(
        flags,
        *[
            in_hbm(v)
            for v in (
                x, jacobian, rhs, well_coupling,
                perf_block.reshape(1, perfs), perf_well.reshape(1, perfs),
                perf_owner.reshape(1, perfs), well_rhs, well_inverse,
            )
        ],
    )

    def add(kept, own, got):
        return pl.pallas_call(
            functools.partial(add_kernel, base),
            out_shape=shape(*own.shape),
            in_specs=[VM] * 3,
            out_specs=VM,
            compiler_params=PARAMS,
            name="add",
        )(kept, own, got)

    def inner_first(x, jac, rhs, jac_part, own_half):
        return pl.pallas_call(
            functools.partial(inner_kernel, True),
            out_shape=(
                grid,
                shape(*jac.shape),
                shape(*jac.shape, dtype=BF16),
                shape(WELL_UNK, PHASES, perfs, LANES, dtype=BF16),
                grid,
            ),
            in_specs=[VM, HB, VM, VM, HB, HB, VM],
            out_specs=(VM,) * 5,
            scratch_shapes=[
                pltpu.VMEM(cell_coupling.shape, BF16),
                pltpu.SemaphoreType.DMA((rows,)),
            ],
            input_output_aliases={3: 2},
            compiler_params=PARAMS,
            name="inner_widen",
        )(x, in_hbm(jac), rhs, jac_part, in_hbm(cell_coupling), in_hbm(diag), own_half)

    inner = pl.pallas_call(
        functools.partial(inner_kernel, False),
        out_shape=grid,
        in_specs=[VM] * 3,
        out_specs=VM,
        compiler_params=PARAMS,
        name="inner",
    )
    work = [
        pltpu.VMEM((PHASES, perfs, 2 * LANES), BF16),
    ]
    for sweep in range(ITERS):
        last = sweep == ITERS - 1
        g1 = lax.ppermute(m1, "gy", gy_swap(gy, 0))
        g3 = lax.ppermute(m3, both, gx_swap(gx, gy, 0))
        g4 = lax.ppermute(m4, both, gx_swap(gx, gy, 1))
        own = add(m2_halo, m1, g1)
        g2 = lax.ppermute(own, "gy", gy_swap(gy, 1))
        hop = 4
        while hop < gy:
            own = jnp.concatenate([own[:base], own[base:] + g2[base:]], axis=0)
            far = lax.ppermute(own[base:], "gy", [(j, (j + hop) % gy) for j in range(gy)])
            g2 = jnp.concatenate([g2[:base], far], axis=0)
            hop *= 2
        if sweep == 0:
            wconst = own[full:] + g2[full:]
            own, g1, g2 = own[:full], g1[:full], g2[:full]
        if sweep == 0:
            z, jac, _, cc, inv = inner_first(x, jacobian, rhs, jac_part, own_half)
        else:
            z = inner(x, jac, rhs)
        operands = (flags, z, own, g1, g2, g3, g4, wconst, inv, spread, well_hot, cc)
        if last:
            x, adj = pl.pallas_call(
                functools.partial(update_kernel, True),
                out_shape=(grid, shape(*well_rhs.shape)),
                in_specs=[SM] + [VM] * 11,
                out_specs=(HB, VM),
                scratch_shapes=work
                + [
                    pltpu.VMEM((phases, cells, layers), F32),
                    pltpu.SemaphoreType.DMA((PHASES,)),
                ],
                compiler_params=PARAMS,
                name="update_last",
            )(*operands)
        else:
            x, m1_halo, m2_halo, m3, m4 = pl.pallas_call(
                functools.partial(update_kernel, False),
                out_shape=(
                    shape(phases, cells, layers),
                    shape(base, LANES),
                    shape(base, LANES),
                    shape(PHASES * cols, LANES),
                    shape(PHASES * cols, LANES),
                ),
                in_specs=[SM] + [VM] * 13,
                out_specs=(VM,) * 5,
                scratch_shapes=work,
                compiler_params=PARAMS,
                name="update",
            )(*operands, row_edges, col_edges)
            m1, m4 = pl.pallas_call(
                wells_kernel,
                out_shape=(shape(full, LANES), shape(*m4.shape)),
                in_specs=[VM] * 6,
                out_specs=(VM,) * 2,
                scratch_shapes=[
                    pltpu.VMEM((PHASES, cells, 2 * LANES), BF16),
                    pltpu.VMEM((PHASES, perfs, LANES), F32),
                ],
                compiler_params=PARAMS,
                name="wells",
            )(x, pick, well_hot, wc, m1_halo, m4)
    return x.reshape(adjoint_init.shape), adj


def solution(mesh):
    in_specs = (
        P(None, "gx", "gy", None),
        P(None, "gx", "gy", None),
        P(None, None, None, "gx", "gy", None),
        P(None, "gx", "gy", None),
        P(("gx", "gy"), None),
        P(("gx", "gy")),
        P(("gx", "gy")),
        P(None, None, ("gx", "gy")),
        P(None, None, ("gx", "gy")),
        P(None, ("gx", "gy")),
        P(None, None, ("gx", "gy")),
    )
    out_specs = (P(None, "gx", "gy", None), P(None, ("gx", "gy")))
    return jax.shard_map(body, mesh=mesh, in_specs=in_specs, out_specs=out_specs, check_vma=False)
```

```python
import functools

import jax
import jax.numpy as jnp
from jax import lax
from jax.experimental import pallas as pl
from jax.experimental.pallas import tpu as pltpu
from jax.sharding import PartitionSpec as P

PHASES = 3
WELL_UNK = 4
BLOCK = 64
ITERS = 8
LANES = 128
F32 = jnp.float32
BF16 = jnp.bfloat16
VM = pl.BlockSpec(memory_space=pltpu.VMEM)
HB = pl.BlockSpec(memory_space=pltpu.MemorySpace.HBM)
SM = pl.BlockSpec(memory_space=pltpu.SMEM)
PARAMS = pltpu.CompilerParams(vmem_limit_bytes=16 * 1024 * 1024)


def split_2(value):
    high = value.astype(BF16)
    return high, (value - high.astype(F32)).astype(BF16)


def edge_messages(flags, x_ref, row_ref, col_ref, m1_ref, m2_ref, m3_ref, m4_ref):
    rows, cols = col_ref.shape[3], row_ref.shape[3]
    gx_odd, gy_odd = flags[0] == 1, flags[1] == 1
    x_first = [x_ref[r, 0:cols, :] for r in range(PHASES)]
    x_last = [x_ref[r, (rows - 1) * cols : rows * cols, :] for r in range(PHASES)]
    c_first = [x_ref[r, pl.ds(0, rows, stride=cols), :] for r in range(PHASES)]
    c_last = [x_ref[r, pl.ds(cols - 1, rows, stride=cols), :] for r in range(PHASES)]
    for t in range(PHASES):
        up = sum(row_ref[0, r, t] * x_first[r] for r in range(PHASES))
        down = sum(row_ref[1, r, t] * x_last[r] for r in range(PHASES))
        left = sum(col_ref[0, r, t] * c_first[r] for r in range(PHASES))
        right = sum(col_ref[1, r, t] * c_last[r] for r in range(PHASES))
        m3_ref[t * cols : (t + 1) * cols, :] = jnp.where(gx_odd, up, down)
        m4_ref[t * cols : (t + 1) * cols, :] = jnp.where(gx_odd, down, up)
        m1_ref[t * rows : (t + 1) * rows, :] = jnp.where(gy_odd, left, right)
        m2_ref[t * rows : (t + 1) * rows, :] = jnp.where(gy_odd, right, left)


def picked_rows(r, x_ref, pick_ref, xs_ref, g_ref):
    high, low = split_2(x_ref[r])
    xs_ref[r, :, 0:LANES] = high
    xs_ref[r, :, LANES : 2 * LANES] = low
    both = jnp.dot(pick_ref[...], xs_ref[r], preferred_element_type=F32)
    g_ref[r] = both[:, 0:LANES] + both[:, LANES:]


def well_partials(pick_ref, well_ref, wc_ref, g_ref, write):
    perfs = pick_ref.shape[0]
    width = well_ref.shape[0]
    chunk = 64
    totals = [[jnp.zeros((8, LANES), F32) for _ in range(width)] for _ in range(WELL_UNK)]
    for start in range(0, perfs, chunk):
        rows = slice(start, start + chunk)
        picked = [g_ref[r, rows, :] for r in range(PHASES)]
        for u in range(WELL_UNK):
            lane_terms = sum(wc_ref[u, r, rows].astype(F32) * picked[r] for r in range(PHASES))
            term = jnp.sum(lane_terms, axis=1, keepdims=True)
            for h in range(width):
                spread = well_ref[h, rows, :] * term
                totals[u][h] = totals[u][h] + sum(spread[i : i + 8] for i in range(0, chunk, 8))
    for h in range(width):
        for u in range(WELL_UNK):
            write(h * WELL_UNK + u, jnp.sum(totals[u][h], axis=0, keepdims=True))


def expanded(eye, coupling_ref, u, own_half, out_ref):
    for r in range(PHASES):
        piece = coupling_ref[u, r * BLOCK : (r + 1) * BLOCK, :]
        doubled = jnp.concatenate([piece, piece], axis=0)
        out_ref[u, r] = jnp.where(own_half, turned(eye, doubled), 0.0).astype(BF16)


def turned(eye, value):
    return lax.dot_general(eye, value, (((1,), (1,)), ((), ())), preferred_element_type=F32)


def hot(mask):
    return mask.astype(F32).astype(BF16)


def iota(dims, axis):
    return lax.broadcasted_iota(jnp.int32, dims, axis)


def first_kernel(
    flags, x_in, jac_in, rhs_in, wcoef_in,
    block_in, well_in, owner_in, rhs_well_in, inv_well_in,
    x_ref, jac_ref, rhs_ref, row_ref, col_ref, pick_ref, spread_ref, well_ref, wc_ref,
    half_ref, m1_ref, m2_ref, m3_ref, m4_ref, wcoef, xs_ref, g_ref,
    block_row, well_row, owner_row, rhs_well, inv_well, row_raw, col_raw, held, sems, small_sems,
):
    rows, cols = jac_in.shape[3], jac_in.shape[4]
    early = rows // 4 + 3
    pairs = [
        (block_in, block_row), (well_in, well_row), (owner_in, owner_row),
        (rhs_well_in, rhs_well), (inv_well_in, inv_well),
    ]
    small = [pltpu.make_async_copy(a, b, small_sems.at[i]) for i, (a, b) in enumerate(pairs)]
    for copy in small:
        copy.start()
    pairs = [
        (wcoef_in, wcoef), (x_in, x_ref),
        (jac_in.at[1, :, :, 0], row_raw.at[0]),
        (jac_in.at[2, :, :, rows - 1], row_raw.at[1]),
        (jac_in.at[3, :, :, :, 0:8], col_raw.at[0]),
        (jac_in.at[4, :, :, :, cols - 8 : cols], col_raw.at[1]),
        (jac_in.at[:, :, :, rows - 1], jac_ref.at[:, :, :, rows - 1]),
        (jac_in.at[:, :, :, 0:early], jac_ref.at[:, :, :, 0:early]), (rhs_in, rhs_ref),
    ]
    copies = [pltpu.make_async_copy(a, b, sems.at[i]) for i, (a, b) in enumerate(pairs)]
    for copy in copies:
        copy.start()
    cells = rows * cols
    perfs = block_row.shape[1]
    width = well_ref.shape[0]
    well_dev = rhs_well.shape[1]
    base, unk = PHASES * rows, WELL_UNK * width
    eye = hot(iota((perfs, perfs), 0) == iota((perfs, perfs), 1))
    for copy in small:
        copy.wait()
    block = block_row[...]
    spread = hot(iota((cells, perfs), 0) == block // 2)
    spread_ref[...] = spread
    pick = turned(eye, spread).astype(BF16)
    pick_ref[...] = pick
    half_ref[...] = turned(eye, hot(iota((LANES, perfs), 0) // BLOCK == block % 2))
    own_half = half_ref[...] > 0.5
    for h in range(width):
        slot = iota((LANES, perfs), 0) + h * LANES
        well = owner_row[...] * well_dev + well_row[...]
        well_ref[h] = turned(eye, hot(slot == well))
    held[...] = jnp.zeros_like(held)
    held[0:WELL_UNK, 0:well_dev] = rhs_well[...]
    for v in range(WELL_UNK):
        held[(v + 1) * WELL_UNK : (v + 2) * WELL_UNK, 0:well_dev] = inv_well[v]
    own_lane = flags[4] * well_dev
    placed = pltpu.roll(held[...], own_lane % LANES, 1)
    for h in range(width):
        value = jnp.where(own_lane // LANES == h, placed, 0.0)
        at = base + unk + h * WELL_UNK
        m1_ref[at : at + WELL_UNK, :] = value[0:WELL_UNK]
        at = base + 2 * unk + h * WELL_UNK * WELL_UNK
        m1_ref[at : at + WELL_UNK * WELL_UNK, :] = value[WELL_UNK : 5 * WELL_UNK]
    for copy in copies[0:6]:
        copy.wait()
    for u in range(WELL_UNK):
        expanded(eye, wcoef, u, own_half, wc_ref)

    def write(row, value):
        m1_ref[base + row : base + row + 1, :] = value

    for r in range(PHASES):
        picked_rows(r, x_ref, pick_ref, xs_ref, g_ref)
    well_partials(pick_ref, well_ref, wc_ref, g_ref, write)
    row_ref[...] = row_raw[...].astype(F32)
    for r in range(PHASES):
        for t in range(PHASES):
            for i in range(rows):
                col_ref[0, r, t, i : i + 1, :] = col_raw[0, r, t, i].astype(F32)[0:1]
                col_ref[1, r, t, i : i + 1, :] = col_raw[1, r, t, i].astype(F32)[7:8]
    edge_messages(flags, x_ref, row_ref, col_ref, m1_ref, m2_ref, m3_ref, m4_ref)
    for copy in copies[6:]:
        copy.wait()


def add_kernel(base, kept_ref, own_ref, got_ref, out_ref):
    out_ref[0:base, :] = kept_ref[...]
    out_ref[base:, :] = own_ref[base:, :] + got_ref[base:, :]


def inner_kernel(widen, x_ref, jac_in, rhs_ref, *rest):
    rows, cols = jac_in.shape[3], jac_in.shape[4]
    early = rows // 4 + 3
    z_ref = rest[0]
    if widen:
        ccoef_in, diag_in, half_ref, z_ref, wide_ref, jac_ref, cc_ref, inv_ref, ccoef, sems = rest[1:]

        def fetch(row):
            return pltpu.make_async_copy(
                jac_in.at[:, :, :, row], jac_ref.at[:, :, :, row], sems.at[row]
            )

        for row in range(early, rows - 1):
            fetch(row).start()
        extra = [
            pltpu.make_async_copy(ccoef_in, ccoef, sems.at[0]),
            pltpu.make_async_copy(diag_in, inv_ref, sems.at[1]),
        ]
        for copy in extra:
            copy.start()
    else:
        jac_ref = jac_in
    lane, col = iota((cols, LANES), 1), iota((cols, LANES), 0)

    def row_body(i, carry):
        if widen:
            pl.when((i + 1 >= early) & (i < rows - 2))(lambda: fetch(i + 1).wait())
        before = jnp.where(i == 0, rows - 1, i - 1)
        after = jnp.where(i == rows - 1, 0, i + 1)
        open_row = {1: (after > 0).astype(F32), 2: (before < rows - 1).astype(F32)}
        shut_cell = {
            3: col == 0, 4: col == cols - 1, 5: lane == 0, 6: lane == LANES - 1
        }

        def load(row):
            start = pl.multiple_of(row * cols, cols)
            return [x_ref[r, pl.ds(start, cols), :] for r in range(PHASES)]

        def coefficient(d, r, t, row):
            if not widen:
                return jac_ref[d, r, t, row]
            value = jac_ref[d, r, t, row].astype(F32)
            if d in open_row:
                value = value * open_row[d]
            if d in shut_cell:
                value = jnp.where(shut_cell[d], 0.0, value)
            wide_ref[d, r, t, row] = value
            return value

        def term(d, t, row, values):
            return sum(coefficient(d, r, t, row) * values[r] for r in range(PHASES))

        here, values_before, values_after = load(i), load(before), load(after)
        start = pl.multiple_of(i * cols, cols)
        for t in range(PHASES):
            total = term(0, t, i, here)
            total = total + term(1, t, after, values_after)
            total = total + term(2, t, before, values_before)
            total = total + pltpu.roll(term(3, t, i, here), cols - 1, 0)
            total = total + pltpu.roll(term(4, t, i, here), 1, 0)
            total = total + pltpu.roll(term(5, t, i, here), LANES - 1, 1)
            total = total + pltpu.roll(term(6, t, i, here), 1, 1)
            z_ref[t, pl.ds(start, cols), :] = rhs_ref[t, pl.ds(start, cols), :] - total
        return carry

    lax.fori_loop(0, rows, row_body, 0, unroll=1 if widen else 2)
    if widen:
        perfs = half_ref.shape[0]
        eye = hot(iota((perfs, perfs), 0) == iota((perfs, perfs), 1))
        for copy in extra:
            copy.wait()
        for u in range(WELL_UNK):
            expanded(eye, ccoef, u, half_ref[...] > 0.5, cc_ref)
        inv_ref[...] = 1.0 / inv_ref[...]


def update_kernel(
    last, flags, z_ref, own, g1, g2, g3, g4, wconst, inv_ref, spread_ref, well_ref, cc_ref,
    *rest,
):
    if last:
        x_out, adj_ref, rs_ref, x_ref, sems = rest
    else:
        (row_ref, col_ref, x_ref, m1_ref, m2_ref, m3_ref, m4_ref, rs_ref) = rest
    cells, perfs = spread_ref.shape
    rows = (own.shape[0] - WELL_UNK * well_ref.shape[0]) // PHASES
    cols = cells // rows
    base = PHASES * rows
    width = well_ref.shape[0]
    unk = WELL_UNK * width
    terms = own[base : base + unk, :] + g2[base : base + unk, :]
    left = wconst[0:unk, :] - terms
    solved = []
    for h in range(width):
        value = 0.0
        for v in range(WELL_UNK):
            at = unk + (h * WELL_UNK + v) * WELL_UNK
            at_v = h * WELL_UNK + v
            value = value + wconst[at : at + WELL_UNK, :] * left[at_v : at_v + 1, :]
        solved.append(value)
    chunk = 64
    for start in range(0, perfs, chunk):
        part = slice(start, start + chunk)
        value = [0.0] * PHASES
        for u in range(WELL_UNK):
            chosen = sum(well_ref[h, part, :] * solved[h][u : u + 1, :] for h in range(width))
            factor = jnp.sum(chosen, axis=1, keepdims=True)
            for r in range(PHASES):
                value[r] = value[r] + cc_ref[u, r, part].astype(F32) * factor
        for r in range(PHASES):
            high, low = split_2(value[r])
            rs_ref[r, part, 0:LANES] = high
            rs_ref[r, part, LANES : 2 * LANES] = low
    gx_odd, gy_odd = flags[0] == 1, flags[1] == 1
    gx_open, gy_open = flags[2].astype(F32), flags[3].astype(F32)
    copies = []
    for t in range(PHASES):
        both = jnp.dot(spread_ref[...], rs_ref[t], preferred_element_type=F32)
        x_ref[t] = (z_ref[t] - both[:, 0:LANES] - both[:, LANES:]) * inv_ref[t]
        near, far = g3[t * cols : (t + 1) * cols, :], g4[t * cols : (t + 1) * cols, :] * gx_open
        first, final = slice(0, cols), slice((rows - 1) * cols, rows * cols)
        x_ref[t, first, :] = x_ref[t, first, :] - inv_ref[t, first, :] * jnp.where(gx_odd, near, far)
        x_ref[t, final, :] = x_ref[t, final, :] - inv_ref[t, final, :] * jnp.where(gx_odd, far, near)
        near, far = g1[t * rows : (t + 1) * rows, :], g2[t * rows : (t + 1) * rows, :] * gy_open
        first, final = pl.ds(0, rows, stride=cols), pl.ds(cols - 1, rows, stride=cols)
        x_ref[t, first, :] = x_ref[t, first, :] - inv_ref[t, first, :] * jnp.where(gy_odd, near, far)
        x_ref[t, final, :] = x_ref[t, final, :] - inv_ref[t, final, :] * jnp.where(gy_odd, far, near)
        if last:
            copies.append(pltpu.make_async_copy(x_ref.at[t], x_out.at[t], sems.at[t]))
            copies[t].start()
    if last:
        well_dev = adj_ref.shape[1]
        mine = 0.0
        for h in range(width):
            place = iota((LANES, well_dev), 1) + flags[4] * well_dev
            place = (place == iota((LANES, well_dev), 0) + h * LANES).astype(F32)
            mine = mine + jnp.dot(
                solved[h], place, precision=lax.Precision.HIGHEST, preferred_element_type=F32
            )
        adj_ref[...] = mine
    for copy in copies:
        copy.wait()
    if not last:
        edge_messages(flags, x_ref, row_ref, col_ref, m1_ref, m2_ref, m3_ref, m4_ref)


def wells_kernel(
    x_ref, pick_ref, well_ref, wc_ref, halo_ref, pass_ref, m1_ref, passed_ref, xs_ref, g_ref
):
    base = halo_ref.shape[0]
    m1_ref[0:base, :] = halo_ref[...]
    passed_ref[...] = pass_ref[...]
    for t in range(PHASES):
        picked_rows(t, x_ref, pick_ref, xs_ref, g_ref)

    def write(row, value):
        m1_ref[base + row : base + row + 1, :] = value

    well_partials(pick_ref, well_ref, wc_ref, g_ref, write)


def gx_swap(gx, gy, parity):
    pairs = []
    for i in range(gx):
        k = i ^ 1 if parity == 0 else ((i + 1) ^ 1) - 1
        for j in range(gy):
            pairs.append((i * gy + j, k * gy + j if 0 <= k < gx else i * gy + (j ^ 1)))
    return pairs


def gy_swap(gy, parity):
    if parity == 0:
        return [(j, j ^ 1) for j in range(gy)]
    return [(j, (((j + 1) ^ 1) - 1) % gy) for j in range(gy)]


def in_hbm(value):
    return pltpu.with_memory_space_constraint(value, pltpu.MemorySpace.HBM)


def shape(*dims, dtype=F32):
    return jax.ShapeDtypeStruct(dims, dtype)


def body(
    adjoint_init, adjoint_rhs, jacobian, cell_diag, perf_owner, perf_well, perf_block,
    well_coupling, cell_coupling, well_rhs, well_inverse,
):
    gx, gy = lax.axis_size("gx"), lax.axis_size("gy")
    ix, iy = lax.axis_index("gx"), lax.axis_index("gy")
    phases, rows, cols, layers = adjoint_init.shape
    cells = rows * cols
    perfs = perf_well.shape[0]
    well_dev = well_rhs.shape[1]
    width = gy * well_dev // LANES
    unk = WELL_UNK * width
    base = PHASES * rows
    both = ("gx", "gy")
    flags = jnp.stack(
        [
            ix % 2,
            iy % 2,
            jnp.where(ix % 2 == 1, ix < gx - 1, ix > 0).astype(jnp.int32),
            jnp.where(iy % 2 == 1, iy < gy - 1, iy > 0).astype(jnp.int32),
            iy,
        ]
    ).astype(jnp.int32)
    x = adjoint_init.reshape(phases, cells, layers)
    rhs = adjoint_rhs.reshape(phases, cells, layers)
    diag = cell_diag.reshape(phases, cells, layers)
    full = base + unk
    grid = shape(phases, cells, layers)
    first = pl.pallas_call(
        first_kernel,
        out_shape=(
            grid,
            shape(*jacobian.shape, dtype=BF16),
            grid,
            shape(2, PHASES, PHASES, cols, LANES),
            shape(2, PHASES, PHASES, rows, LANES),
            shape(perfs, cells, dtype=BF16),
            shape(cells, perfs, dtype=BF16),
            shape(width, perfs, LANES),
            shape(WELL_UNK, PHASES, perfs, LANES, dtype=BF16),
            shape(perfs, LANES),
            shape(full + 5 * unk, LANES),
            shape(base, LANES),
            shape(PHASES * cols, LANES),
            shape(PHASES * cols, LANES),
        ),
        in_specs=[SM] + [HB] * 9,
        out_specs=(VM,) * 14,
        scratch_shapes=[
            pltpu.VMEM(well_coupling.shape, BF16),
            pltpu.VMEM((PHASES, cells, 2 * LANES), BF16),
            pltpu.VMEM((PHASES, perfs, LANES), F32),
            pltpu.VMEM((1, perfs), jnp.int32),
            pltpu.VMEM((1, perfs), jnp.int32),
            pltpu.VMEM((1, perfs), jnp.int32),
            pltpu.VMEM(well_rhs.shape, F32),
            pltpu.VMEM(well_inverse.shape, F32),
            pltpu.VMEM((2, PHASES, PHASES, cols, LANES), BF16),
            pltpu.VMEM((2, PHASES, PHASES, rows, 8, LANES), BF16),
            pltpu.VMEM((24, LANES), F32),
            pltpu.SemaphoreType.DMA((9,)),
            pltpu.SemaphoreType.DMA((5,)),
        ],
        compiler_params=PARAMS,
        name="first",
    )
    (x, jac_part, rhs, row_edges, col_edges, pick, spread, well_hot, wc, own_half, m1, m2_halo, m3,
     m4) = first(
        flags,
        *[
            in_hbm(v)
            for v in (
                x, jacobian, rhs, well_coupling,
                perf_block.reshape(1, perfs), perf_well.reshape(1, perfs),
                perf_owner.reshape(1, perfs), well_rhs, well_inverse,
            )
        ],
    )

    def add(kept, own, got):
        return pl.pallas_call(
            functools.partial(add_kernel, base),
            out_shape=shape(*own.shape),
            in_specs=[VM] * 3,
            out_specs=VM,
            compiler_params=PARAMS,
            name="add",
        )(kept, own, got)

    def inner_first(x, jac, rhs, jac_part, own_half):
        return pl.pallas_call(
            functools.partial(inner_kernel, True),
            out_shape=(
                grid,
                shape(*jac.shape),
                shape(*jac.shape, dtype=BF16),
                shape(WELL_UNK, PHASES, perfs, LANES, dtype=BF16),
                grid,
            ),
            in_specs=[VM, HB, VM, VM, HB, HB, VM],
            out_specs=(VM,) * 5,
            scratch_shapes=[
                pltpu.VMEM(cell_coupling.shape, BF16),
                pltpu.SemaphoreType.DMA((rows,)),
            ],
            input_output_aliases={3: 2},
            compiler_params=PARAMS,
            name="inner_widen",
        )(x, in_hbm(jac), rhs, jac_part, in_hbm(cell_coupling), in_hbm(diag), own_half)

    inner = pl.pallas_call(
        functools.partial(inner_kernel, False),
        out_shape=grid,
        in_specs=[VM] * 3,
        out_specs=VM,
        compiler_params=PARAMS,
        name="inner",
    )
    work = [
        pltpu.VMEM((PHASES, perfs, 2 * LANES), BF16),
    ]
    for sweep in range(ITERS):
        last = sweep == ITERS - 1
        g1 = lax.ppermute(m1, "gy", gy_swap(gy, 0))
        g3 = lax.ppermute(m3, both, gx_swap(gx, gy, 0))
        g4 = lax.ppermute(m4, both, gx_swap(gx, gy, 1))
        own = add(m2_halo, m1, g1)
        g2 = lax.ppermute(own, "gy", gy_swap(gy, 1))
        hop = 4
        while hop < gy:
            own = jnp.concatenate([own[:base], own[base:] + g2[base:]], axis=0)
            far = lax.ppermute(own[base:], "gy", [(j, (j + hop) % gy) for j in range(gy)])
            g2 = jnp.concatenate([g2[:base], far], axis=0)
            hop *= 2
        if sweep == 0:
            wconst = own[full:] + g2[full:]
            own, g1, g2 = own[:full], g1[:full], g2[:full]
        if sweep == 0:
            z, jac, _, cc, inv = inner_first(x, jacobian, rhs, jac_part, own_half)
        else:
            z = inner(x, jac, rhs)
        operands = (flags, z, own, g1, g2, g3, g4, wconst, inv, spread, well_hot, cc)
        if last:
            x, adj = pl.pallas_call(
                functools.partial(update_kernel, True),
                out_shape=(grid, shape(*well_rhs.shape)),
                in_specs=[SM] + [VM] * 11,
                out_specs=(HB, VM),
                scratch_shapes=work
                + [
                    pltpu.VMEM((phases, cells, layers), F32),
                    pltpu.SemaphoreType.DMA((PHASES,)),
                ],
                compiler_params=PARAMS,
                name="update_last",
            )(*operands)
        else:
            x, m1_halo, m2_halo, m3, m4 = pl.pallas_call(
                functools.partial(update_kernel, False),
                out_shape=(
                    shape(phases, cells, layers),
                    shape(base, LANES),
                    shape(base, LANES),
                    shape(PHASES * cols, LANES),
                    shape(PHASES * cols, LANES),
                ),
                in_specs=[SM] + [VM] * 13,
                out_specs=(VM,) * 5,
                scratch_shapes=work,
                compiler_params=PARAMS,
                name="update",
            )(*operands, row_edges, col_edges)
            m1, m4 = pl.pallas_call(
                wells_kernel,
                out_shape=(shape(full, LANES), shape(*m4.shape)),
                in_specs=[VM] * 6,
                out_specs=(VM,) * 2,
                scratch_shapes=[
                    pltpu.VMEM((PHASES, cells, 2 * LANES), BF16),
                    pltpu.VMEM((PHASES, perfs, LANES), F32),
                ],
                compiler_params=PARAMS,
                name="wells",
            )(x, pick, well_hot, wc, m1_halo, m4)
    return x.reshape(adjoint_init.shape), adj


def solution(mesh):
    in_specs = (
        P(None, "gx", "gy", None),
        P(None, "gx", "gy", None),
        P(None, None, None, "gx", "gy", None),
        P(None, "gx", "gy", None),
        P(("gx", "gy"), None),
        P(("gx", "gy")),
        P(("gx", "gy")),
        P(None, None, ("gx", "gy")),
        P(None, None, ("gx", "gy")),
        P(None, ("gx", "gy")),
        P(None, None, ("gx", "gy")),
    )
    out_specs = (P(None, "gx", "gy", None), P(None, ("gx", "gy")))
    return jax.shard_map(body, mesh=mesh, in_specs=in_specs, out_specs=out_specs, check_vma=False)
```
